128 devices in a mesh: ctx: 16 (over x_lo, z, core), ch: 4 (over y), rep: 2 (over x_hi).
Axes of the slice: x: 4 (x_hi: 2, x_lo: 2; x = x_hi * 2 + x_lo), y: 4, z: 4, core: 2. Of those that a mesh axis runs over, the one named last changes fastest.
Arguments:
- saved_input: bfloat16 [2, 8192, 8192], P('rep', 'ctx', 'ch'), may hold values from -6 to 6
- out_grad: bfloat16 [2, 8192, 8192], P('rep', 'ctx', 'ch'), may hold values from -6 to 6
- filter_taps: bfloat16 [256, 8192], P('ctx', 'ch'), may hold values from -0.375 to 0.375
- valid_counts: int32 [2, 16], P('rep', 'ctx'), may hold values from 128 to 512
Outputs:
- input_grad: bfloat16 [2, 8192, 8192], P('rep', 'ctx', 'ch')
- tap_grad: float32 [256, 8192], P('ctx', 'ch')
The draws below stay inside these ranges and needn't reach their ends.
Inputs may be any that keep to these rules, and one draw needn't show every extreme that they name: `valid_counts`: positions of a block at local index below its count are live; the others carry no gradient.
All inputs are finite; a program needn't handle non-finite values.
Results may differ from the reference program's by a relative error of at most 0.001.
Values may be sent and summed in bfloat16 or wider, within the bound.
A program may use at most 128 MiB of HBM per device.

```python
import math
import jax
import jax.numpy as jnp
from jax import lax

C = 8192
REACH = 128
T_DEV = 512
TAPS = 256
LENGTH = 8192
ALL_ROWS = 16384
N_CTX = 16
N_REP = 2


def set_ends(values, key, smallest, top_value):
    extent = values.shape
    place = [jax.random.randint(jax.random.fold_in(key, axis), (), 0, extent[axis]) for axis in range(len(extent))]
    values = values.at[tuple(place)].set(smallest)
    longest = extent.index(max(extent))
    place[longest] = (place[longest] + 1) % extent[longest]
    return values.at[tuple(place)].set(top_value)


def block_levels(stream_key, dims, cuts, smallest, top_value):
    gain, own = 1.0, jax.random.fold_in(stream_key, 6)
    for axis_at, shards_of in cuts:
        heights = jnp.exp(jax.random.uniform(jax.random.fold_in(own, axis_at), (shards_of,), jnp.float32, smallest / len(cuts), top_value / len(cuts)))
        gain = gain * jnp.repeat(heights, dims[axis_at] // shards_of).reshape([-1 if axis == axis_at else 1 for axis in range(len(dims))])
    return gain


def noise(own_key, dims, spread, limit, split=(), kind=jnp.bfloat16):
    result = jax.random.normal(own_key, dims, jnp.float32) * spread
    if len(split) > 0:
        result = block_levels(own_key, dims, split, -0.22, 0.18) * result
    return jnp.clip(result, min=-limit, max=limit).astype(kind)


def setup_inputs(seed: int = 0) -> dict:
    key_list = jax.random.split(jax.random.key(seed), 5)
    return {
        "saved_input": noise(key_list[0], (N_REP, LENGTH, C), 1.0, 6.0, ((0, 2), (1, 16), (2, 4))),
        "out_grad": noise(key_list[1], (N_REP, LENGTH, C), 1.0, 6.0, ((0, 2), (1, 16), (2, 4))),
        "filter_taps": noise(key_list[2], (TAPS, C), TAPS ** -0.5, 0.375, ((0, 16), (1, 4))),
        "valid_counts": set_ends(jax.random.randint(key_list[3], (N_REP, N_CTX), T_DEV // 4, T_DEV + 1), jax.random.fold_in(key_list[3], 1), T_DEV // 4, T_DEV).astype(jnp.int32),
    }


def reference(saved_input, out_grad, filter_taps, valid_counts):
    positions = jnp.arange(LENGTH)
    live_rows = ((positions % T_DEV)[None, :] < valid_counts[:, positions // T_DEV]).astype(jnp.float32)[:, :, None]
    input_live = saved_input.astype(jnp.float32) * live_rows
    grad_live = out_grad.astype(jnp.float32) * live_rows
    fft_size = 1 << (LENGTH + 2 * REACH).bit_length()
    cycle_rows = (REACH - jnp.arange(2 * REACH)) % fft_size
    lags = (jnp.arange(2 * REACH) - REACH) % fft_size
    group = min(512, C)
    count = C // group

    def split_channels(array):
        return jnp.moveaxis(array.reshape(array.shape[:-1] + (count, group)), -2, 0)

    def per_group(parts):
        input_part, grad_part, taps_part = parts
        filter_cycle = jnp.zeros((fft_size, group), jnp.float32).at[cycle_rows].set(taps_part)
        input_hat = jnp.fft.rfft(input_part, fft_size, axis=1)
        grad_hat = jnp.fft.rfft(grad_part, fft_size, axis=1)
        filter_hat = jnp.fft.rfft(filter_cycle, axis=0)
        input_grad = jnp.fft.irfft(grad_hat * filter_hat[None], fft_size, axis=1)[:, :LENGTH]
        lagged = jnp.fft.irfft(grad_hat * jnp.conj(input_hat), fft_size, axis=1).sum(axis=0)
        return (input_grad, lagged[lags])
    input_grads, tap_parts = lax.map(per_group, (split_channels(input_live), split_channels(grad_live), split_channels(filter_taps.astype(jnp.float32))))
    input_grads = jnp.moveaxis(input_grads, 0, -2).reshape(N_REP, LENGTH, C)
    tap_parts = jnp.moveaxis(tap_parts, 0, 1).reshape(2 * REACH, C)
    return ((input_grads * live_rows).astype(jnp.bfloat16), tap_parts * (1.0 / math.sqrt(ALL_ROWS)))
```

```python
import math

import jax
import jax.numpy as jnp
import numpy as np
from jax import lax
from jax.experimental import pallas as pl
from jax.experimental.pallas import tpu as pltpu
from jax.sharding import PartitionSpec as P

REACH = 128
TILE = 256


def transform_tables():
    order = np.concatenate([np.arange(0, 128, 2), np.arange(1, 128, 2)])
    turns = (2 * order[:, None] + 1) * np.arange(128)[None, :] % 512
    angle = np.pi * turns / 256.0
    forward = np.concatenate([np.cos(angle), -np.sin(angle)], 0)
    high = forward.astype(jnp.bfloat16)
    low = (forward - high.astype(np.float64)).astype(jnp.bfloat16)
    analysis = np.concatenate([high, low], 1)
    inv_high = (high.astype(np.float64).T / 128).astype(jnp.bfloat16)
    inv_low = (low.astype(np.float64).T / 128).astype(jnp.bfloat16)
    synthesis = np.concatenate([inv_high, inv_high, inv_low], 1)
    return analysis, synthesis


def split(value):
    high = value.astype(jnp.bfloat16)
    low = (value - high.astype(jnp.float32)).astype(jnp.bfloat16)
    return high, low


def kernel(count_ref, ana_ref, syn_ref, x_ref, g_ref, left_ref, right_ref, w_ref,
           out_ref, tap_ref, a_ref, xf_ref, wf_ref, y_ref, t_ref):
    live_count = count_ref[0, 0]
    ana = ana_ref[...]
    syn = syn_ref[...]

    def analyse(block):
        return jnp.dot(ana, jnp.concatenate([block, block], 0), preferred_element_type=jnp.float32)

    def live_rows(b):
        rows = lax.broadcasted_iota(jnp.int32, (REACH, TILE), 0) + b * REACH
        return rows < live_count

    a_ref[0] = analyse(left_ref[...])
    a_ref[5] = analyse(right_ref[...])
    for b in range(4):
        live = live_rows(b)
        rows = pl.ds(b * REACH, REACH)
        a_ref[b + 1] = analyse(jnp.where(live, g_ref[rows, :], 0))
        xf_ref[b] = analyse(jnp.where(live, x_ref[rows, :], 0))
    for h in range(2):
        wf_ref[h] = analyse(w_ref[pl.ds(h * REACH, REACH), :])

    step = 16
    for chunk in range(128 // step):
        re = pl.ds(chunk * step, step)
        im = pl.ds(128 + chunk * step, step)
        positive = chunk * step < 64
        ar = [a_ref[b, re, :] for b in range(6)]
        ai = [a_ref[b, im, :] for b in range(6)]
        gr, gi = [], []
        for b in range(5):
            if positive:
                gr.append(ar[b] + ai[b + 1])
                gi.append(ai[b] - ar[b + 1])
            else:
                gr.append(ar[b] - ai[b + 1])
                gi.append(ai[b] + ar[b + 1])
        for h in range(2):
            tr = ti = None
            for b in range(4):
                xr, xi = xf_ref[b, re, :], xf_ref[b, im, :]
                pr = xr * gr[b + h] + xi * gi[b + h]
                pi = xr * gi[b + h] - xi * gr[b + h]
                tr, ti = (pr, pi) if tr is None else (tr + pr, ti + pi)
            for rows, val in ((chunk * step, tr), (128 + chunk * step, ti)):
                high, low = split(val)
                t_ref[h, pl.ds(rows, step), :] = high
                t_ref[h, pl.ds(256 + rows, step), :] = low
                t_ref[h, pl.ds(512 + rows, step), :] = high
        w0r, w0i = wf_ref[0, re, :], wf_ref[0, im, :]
        w1r, w1i = wf_ref[1, re, :], wf_ref[1, im, :]
        for b in range(4):
            yr = (w0r * gr[b] + w0i * gi[b]) + (w1r * gr[b + 1] + w1i * gi[b + 1])
            yi = (w0r * gi[b] - w0i * gr[b]) + (w1r * gi[b + 1] - w1i * gr[b + 1])
            for rows, val in ((chunk * step, yr), (128 + chunk * step, yi)):
                high, low = split(val)
                y_ref[b, pl.ds(rows, step), :] = high
                y_ref[b, pl.ds(256 + rows, step), :] = low
                y_ref[b, pl.ds(512 + rows, step), :] = high

    for h in range(2):
        tap_ref[pl.ds(h * REACH, REACH), :] = jnp.dot(
            syn, t_ref[h], preferred_element_type=jnp.float32) * (1.0 / 128)
    for b in range(4):
        value = jnp.dot(syn, y_ref[b], preferred_element_type=jnp.float32)
        out_ref[pl.ds(b * REACH, REACH), :] = jnp.where(live_rows(b), value, 0).astype(jnp.bfloat16)


def convolve(counts, x, g, left, right, taps):
    rows, channels = x.shape
    ana, syn = transform_tables()
    block = lambda n: pl.BlockSpec((n, TILE), lambda i: (0, i))
    whole = lambda a: pl.BlockSpec(a.shape, lambda i: (0, 0))
    return pl.pallas_call(
        kernel,
        grid=(channels // TILE,),
        out_shape=(jax.ShapeDtypeStruct((rows, channels), jnp.bfloat16),
                   jax.ShapeDtypeStruct((2 * REACH, channels), jnp.float32)),
        in_specs=[pl.BlockSpec(memory_space=pltpu.SMEM), whole(ana), whole(syn),
                  block(rows), block(rows), block(REACH), block(REACH), block(2 * REACH)],
        out_specs=(block(rows), block(2 * REACH)),
        scratch_shapes=[
            pltpu.VMEM((6, 256, TILE), jnp.float32),
            pltpu.VMEM((4, 256, TILE), jnp.float32),
            pltpu.VMEM((2, 256, TILE), jnp.float32),
            pltpu.VMEM((4, 768, TILE), jnp.bfloat16),
            pltpu.VMEM((2, 768, TILE), jnp.bfloat16),
        ],
        compiler_params=pltpu.CompilerParams(vmem_limit_bytes=40 << 20),
    )(counts, jnp.asarray(ana), jnp.asarray(syn), x, g, left, right, taps)


def local(saved_input, out_grad, filter_taps, valid_counts):
    block_rows = saved_input.shape[1]
    count = lax.axis_size("ctx")
    grad = out_grad[0]
    live = (jnp.arange(block_rows) < valid_counts[0, 0])[:, None]
    head = jnp.where(live[:REACH], grad[:REACH], 0)
    tail = jnp.where(live[-REACH:], grad[-REACH:], 0)
    left = lax.ppermute(tail, "ctx", [(i, i + 1) for i in range(count - 1)])
    right = lax.ppermute(head, "ctx", [(i + 1, i) for i in range(count - 1)])
    taps = lax.all_gather(filter_taps, "ctx", axis=0, tiled=True)
    input_grad, tap_terms = convolve(valid_counts, saved_input[0], grad, left, right, taps)
    segment = lax.psum_scatter(tap_terms, "ctx", scatter_dimension=0, tiled=True)
    tap_grad = lax.psum(segment, "rep")
    return (input_grad[None], tap_grad)


def solution(mesh):
    return jax.shard_map(
        local,
        mesh=mesh,
        in_specs=(P("rep", "ctx", "ch"), P("rep", "ctx", "ch"), P("ctx", "ch"), P("rep", "ctx")),
        out_specs=(P("rep", "ctx", "ch"), P("ctx", "ch")),
        check_vma=False,
    )
```

```python
import functools
import math

import jax
import jax.numpy as jnp
import numpy as np
from jax import lax
from jax.experimental import pallas as pl
from jax.experimental.pallas import tpu as pltpu
from jax.sharding import PartitionSpec as P

REACH = 128
TILE = 256
STEP = 16
Z = 4


def transform_tables():
    freq = 2 * np.arange(128)[:, None] + 1
    analysis, synthesis = [], []
    for b in range(4):
        angle = np.pi * (freq * (np.arange(128)[None, :] + 128 * b) % 512) / 256.0
        forward = np.concatenate([np.cos(angle), -np.sin(angle)], 0)
        high = forward.astype(jnp.bfloat16)
        low = (forward - high.astype(np.float64)).astype(jnp.bfloat16)
        analysis.append(np.concatenate([high, low], 1))
        back = [part.astype(np.float64).T / 128 for part in (high, high, low)]
        synthesis.append(np.concatenate(back, 1))
    rows = [32 * z + 16 * core + 8 * half + r
            for core in range(2) for half in range(2) for z in range(Z) for r in range(8)]
    tap_scale = 1.0 / 128
    taps = [synthesis[h][rows] * tap_scale for h in range(2)]
    return (np.stack(analysis), np.stack(synthesis).astype(jnp.bfloat16),
            np.stack(taps).astype(jnp.bfloat16))


def split(value):
    high = value.astype(jnp.bfloat16)
    low = (value - high.astype(jnp.float32)).astype(jnp.bfloat16)
    return high, low


def kernel(tiles, count_ref, ana_ref, syn_ref, tsyn_ref, x_hbm, g_hbm, w_hbm,
           out_hbm, tap_hbm,
           gbuf, xbuf, obuf, from_left, from_right, wbuf,
           af, xf, gf, wf, yf, tf, tap, pair_in, xa_in, xb_in, z_in, fin,
           load_sem, out_sem, halo_s, halo_r, wz_s, wz_r, wx_s, wx_r, wp_s, wp_r,
           p_s, p_r, xa_s, xa_r, xb_s, xb_r, z_s, z_r, h_s, h_r):
    live_count = count_ref[0, 0]
    ctx = lax.axis_index("ctx")
    rep = lax.axis_index("rep")
    ends = 16
    core = lax.rem(ctx, 2)
    z = lax.rem(lax.div(ctx, 2), Z)
    xlo = lax.div(ctx, 8)
    half_cols = tiles * TILE // 2

    def device(x_lo, z_at, core_at, rep_at):
        return {"ctx": x_lo * 8 + z_at * 2 + core_at, "rep": rep_at}

    def remote(src, dst, send, recv, target):
        return pltpu.make_async_remote_copy(
            src_ref=src, dst_ref=dst, send_sem=send, recv_sem=recv,
            device_id=target, device_id_type=pl.DeviceIdType.MESH)

    left = {"ctx": lax.rem(ctx + ends - 1, ends), "rep": rep}
    right = {"ctx": lax.rem(ctx + 1, ends), "rep": rep}
    sibling = device(xlo, z, 1 - core, rep)
    x_near = device(1 - xlo, z, core, rep)
    x_wrap = device(1 - xlo, z, core, 1 - rep)
    x_far = device(xlo, z, core, 1 - rep)
    z_peers = [device(xlo, lax.rem(z + d, Z), core, rep) for d in range(1, Z)]

    barrier = pltpu.get_barrier_semaphore()
    peers = [left, right, x_near, x_wrap, x_far] + z_peers
    for peer in peers:
        pl.semaphore_signal(barrier, inc=1, device_id=peer, device_id_type=pl.DeviceIdType.MESH)

    own_half = pl.ds(pl.multiple_of(rep * half_cols, TILE // 2), half_cols)
    loads = [
        pltpu.make_async_copy(g_hbm.at[0, pl.ds(384, 128), :], gbuf.at[pl.ds(384, 128), :], load_sem.at[0]),
        pltpu.make_async_copy(w_hbm.at[:, own_half], wbuf.at[xlo, z, core, :, own_half], load_sem.at[1]),
        pltpu.make_async_copy(g_hbm.at[0, pl.ds(0, 384), :], gbuf.at[pl.ds(0, 384), :], load_sem.at[2]),
        pltpu.make_async_copy(x_hbm.at[0], xbuf, load_sem.at[3]),
    ]
    for copy in loads:
        copy.start()

    def cols(i):
        return pl.ds(pl.multiple_of(i * TILE, TILE), TILE)

    def live_rows(b):
        rows = lax.broadcasted_iota(jnp.int32, (REACH, TILE), 0) + b * REACH
        return rows < live_count

    def halo_right(i):
        return remote(gbuf.at[pl.ds(384, 128), cols(i)], from_left.at[i],
                      halo_s.at[0, i], halo_r.at[0, i], right)

    def halo_left(i):
        return remote(g_hbm.at[0, pl.ds(0, 128), cols(i)], from_right.at[i],
                      halo_s.at[1, i], halo_r.at[1, i], left)

    def taps_z(d):
        return remote(w_hbm.at[:, own_half], wbuf.at[xlo, z, core, :, own_half],
                      wz_s.at[d], wz_r.at[d], z_peers[d])

    def taps_z_arrival(d):
        source = lax.rem(z + Z - 1 - d, Z)
        return remote(w_hbm.at[:, own_half], wbuf.at[xlo, source, core, :, own_half],
                      wz_s.at[d], wz_r.at[d], z_peers[d])

    def taps_x(d):
        part = wbuf.at[xlo, :, core, :, own_half]
        return remote(part, part, wx_s.at[d], wx_r.at[d], (x_near, x_wrap, x_far)[d])

    def taps_x_arrival(d):
        other_half = pl.ds(pl.multiple_of((1 - rep) * half_cols, TILE // 2), half_cols)
        part = (wbuf.at[1 - xlo, :, core, :, own_half],
                wbuf.at[1 - xlo, :, core, :, other_half],
                wbuf.at[xlo, :, core, :, other_half])[d]
        return remote(part, part, wx_s.at[d], wx_r.at[d], (x_near, x_wrap, x_far)[d])

    def taps_pair(which):
        part = wbuf.at[:, :, which]
        return remote(part, part, wp_s, wp_r, sibling)

    def odd(i):
        return lax.rem(i, 2)

    def keep(i):
        return lax.rem(rep + (1 - odd(i)) * xlo, 2)

    def first_x(i):
        return device(1 - xlo, z, core, lax.rem(rep + odd(i), 2))

    def second_x(i):
        return device(1 - xlo, z, core, lax.rem(rep + 1 - odd(i), 2))

    def pair_copy(i):
        return remote(tap.at[i, 1 - core], pair_in.at[i], p_s.at[i], p_r.at[i], sibling)

    def xa_copy(i):
        return remote(tap.at[i, core, 1 - keep(i)], xa_in.at[i], xa_s.at[i], xa_r.at[i], first_x(i))

    def xb_copy(i):
        return remote(tap.at[i, core, keep(i), 1 - xlo], xb_in.at[i], xb_s.at[i], xb_r.at[i], second_x(i))

    def z_copy(i, d):
        rows = pl.ds(pl.multiple_of(lax.rem(z + 1 + d, Z) * 8, 8), 8)
        return remote(tap.at[i, core, keep(i), xlo, rows, :], z_in.at[i, d],
                      z_s.at[i, d], z_r.at[i, d], z_peers[d])

    def rep_copy(i, which):
        part = fin.at[pl.ds(pl.multiple_of(which * 8, 8), 8), cols(i)]
        return remote(part, part, h_s.at[i], h_r.at[i], x_far)

    def stage_pair(i):
        pair_copy(i).wait_recv()
        tap[i, core] += pair_in[i]
        xa_copy(i).start()

    def stage_xa(i):
        xa_copy(i).wait_recv()
        tap[i, core, keep(i)] += xa_in[i]
        xb_copy(i).start()

    def stage_xb(i):
        xb_copy(i).wait_recv()
        tap[i, core, keep(i), xlo] += xb_in[i]
        for d in range(Z - 1):
            z_copy(i, d).start()

    def stage_z(i):
        for d in range(Z - 1):
            z_copy(i, d).wait_recv()
        mine = tap[i, core, keep(i), xlo, pl.ds(pl.multiple_of(z * 8, 8), 8), :]
        total = (mine + z_in[i, 0]) + (z_in[i, 1] + z_in[i, 2])
        fin[pl.ds(pl.multiple_of(keep(i) * 8, 8), 8), cols(i)] = total
        rep_copy(i, keep(i)).start()

    def reduction(slot):
        for stage, lag in ((stage_z, 7), (stage_xb, 5), (stage_xa, 3), (stage_pair, 1)):
            i = slot - lag

            @pl.when(jnp.logical_and(i >= 0, i < tiles))
            def _(stage=stage, i=i):
                stage(i)

    loads[0].wait()
    tail_live = live_rows(3)

    def mask_tail(i, carry):
        gbuf[pl.ds(384, 128), cols(i)] = jnp.where(tail_live, gbuf[pl.ds(384, 128), cols(i)], 0)
        return carry

    lax.fori_loop(0, tiles, mask_tail, None)
    pl.semaphore_wait(barrier, len(peers))

    def send_halo(i, carry):
        @pl.when(ctx < ends - 1)
        def _():
            halo_right(i).start()

        @pl.when(ctx > 0)
        def _():
            halo_left(i).start()

        return carry

    send_halo(0, None)
    for d in range(Z - 1):
        taps_z(d).start()
    lax.fori_loop(1, tiles, send_halo, None)

    @pl.when(ctx == 0)
    def _():
        from_left[...] = jnp.zeros_like(from_left)

    @pl.when(ctx == ends - 1)
    def _():
        from_right[...] = jnp.zeros_like(from_right)

    for copy in loads[2:]:
        copy.wait()

    def analyse(b, block):
        return jnp.dot(ana_ref[b % 4], jnp.concatenate([block, block], 0),
                       preferred_element_type=jnp.float32)

    def put(ref, at, row, value):
        high, low = split(value)
        ref[at, pl.ds(row, STEP), :] = high
        ref[at, pl.ds(256 + row, STEP), :] = low
        ref[at, pl.ds(512 + row, STEP), :] = high

    def tap_tile(i, carry):
        for b in range(4):
            rows = pl.ds(b * REACH, REACH)
            g_block, x_block = gbuf[rows, cols(i)], xbuf[rows, cols(i)]
            if b > 0:
                x_block = jnp.where(live_rows(b), x_block, 0)
            if b in (1, 2):
                g_block = jnp.where(live_rows(b), g_block, 0)
            af[b + 1] = analyse(b + 1, g_block)
            xf[b] = analyse(b, x_block)

        @pl.when(ctx > 0)
        def _():
            halo_right(i).wait_recv()

        @pl.when(ctx < ends - 1)
        def _():
            halo_left(i).wait_recv()

        af[0] = analyse(0, from_left[i])
        af[5] = analyse(5, from_right[i])

        def chunk(c, carry):
            row = pl.multiple_of(c * STEP, STEP)
            re, im = pl.ds(row, STEP), pl.ds(128 + row, STEP)
            ar = [af[b, re, :] for b in range(6)]
            ai = [af[b, im, :] for b in range(6)]
            gr = [ar[b] + ar[b + 1] for b in range(5)]
            gi = [ai[b] + ai[b + 1] for b in range(5)]
            for b in range(5):
                gf[i, b, re, :] = gr[b]
                gf[i, b, im, :] = gi[b]
            for h in range(2):
                tr = ti = None
                for b in range(4):
                    xr, xi = xf[b, re, :], xf[b, im, :]
                    pr = xr * gr[b + h] + xi * gi[b + h]
                    pi = xr * gi[b + h] - xi * gr[b + h]
                    tr, ti = (pr, pi) if tr is None else (tr + pr, ti + pi)
                put(tf, h, row, tr)
                put(tf, h, 128 + row, ti)
            return carry

        lax.fori_loop(0, 128 // STEP, chunk, None)
        for h in range(2):
            terms = jnp.dot(tsyn_ref[h], tf[h], preferred_element_type=jnp.float32)
            for core_at in range(2):
                for half in range(2):
                    start = (core_at * 2 + half) * 32
                    tap[i, core_at, half, h] = terms[start:start + 32]
        pair_copy(i).start()
        reduction(i)

        @pl.when(i == 0)
        def _():
            loads[1].wait()
            for d in range(Z - 1):
                taps_z_arrival(d).wait_recv()
            for d in range(3):
                taps_x(d).start()

        @pl.when(i == tiles - 2)
        def _():
            for d in range(3):
                taps_x_arrival(d).wait_recv()
            taps_pair(core).start()

        return carry

    lax.fori_loop(0, tiles, tap_tile, None)
    taps_pair(1 - core).wait_recv()

    def store_out(i):
        return pltpu.make_async_copy(obuf.at[:, cols(i)], out_hbm.at[0, :, cols(i)], out_sem.at[i])

    def grad_tile(i, carry):
        for h in range(2):
            block = wbuf[h, :, :, :, cols(i)].reshape(REACH, TILE)
            wf[h] = analyse(h, block)

        def chunk(c, carry):
            row = pl.multiple_of(c * STEP, STEP)
            re, im = pl.ds(row, STEP), pl.ds(128 + row, STEP)
            gr = [gf[i, b, re, :] for b in range(5)]
            gi = [gf[i, b, im, :] for b in range(5)]
            w0r, w0i = wf[0, re, :], wf[0, im, :]
            w1r, w1i = wf[1, re, :], wf[1, im, :]
            for b in range(4):
                yr = (w0r * gr[b] + w0i * gi[b]) + (w1r * gr[b + 1] + w1i * gi[b + 1])
                yi = (w0r * gi[b] - w0i * gr[b]) + (w1r * gi[b + 1] - w1i * gr[b + 1])
                put(yf, b, row, yr)
                put(yf, b, 128 + row, yi)
            return carry

        lax.fori_loop(0, 128 // STEP, chunk, None)
        for b in range(4):
            value = jnp.dot(syn_ref[b], yf[b], preferred_element_type=jnp.float32)
            if b > 0:
                value = jnp.where(live_rows(b), value, 0)
            obuf[pl.ds(b * REACH, REACH), cols(i)] = value.astype(jnp.bfloat16)
        store_out(i).start()
        reduction(i + tiles)
        return carry

    lax.fori_loop(0, tiles, grad_tile, None)
    for slot in range(2 * tiles, tiles + 7):
        reduction(slot)

    def finish(i, carry):
        rep_copy(i, 1 - keep(i)).wait_recv()
        rep_copy(i, keep(i)).wait_send()
        store_out(i).wait()
        pair_copy(i).wait_send()
        xa_copy(i).wait_send()
        xb_copy(i).wait_send()
        for d in range(Z - 1):
            z_copy(i, d).wait_send()

        @pl.when(ctx < ends - 1)
        def _():
            halo_right(i).wait_send()

        @pl.when(ctx > 0)
        def _():
            halo_left(i).wait_send()

        return carry

    lax.fori_loop(0, tiles, finish, None)
    last = pltpu.make_async_copy(fin, tap_hbm, load_sem.at[4])
    last.start()
    for d in range(3):
        taps_z(d).wait_send()
        taps_x(d).wait_send()
    taps_pair(core).wait_send()
    last.wait()


def fused(counts, x, g, taps):
    _, rows, channels = x.shape
    tiles = channels // TILE
    ana, syn, tsyn = transform_tables()
    dma = pltpu.SemaphoreType.DMA
    vmem = pl.BlockSpec(memory_space=pltpu.VMEM)
    hbm = pl.BlockSpec(memory_space=pl.ANY)
    f32, bf16 = jnp.float32, jnp.bfloat16
    return pl.pallas_call(
        functools.partial(kernel, tiles),
        out_shape=(jax.ShapeDtypeStruct(x.shape, bf16),
                   jax.ShapeDtypeStruct(taps.shape, f32)),
        in_specs=[pl.BlockSpec(memory_space=pltpu.SMEM), vmem, vmem, vmem, hbm, hbm, hbm],
        out_specs=(hbm, hbm),
        scratch_shapes=[
            pltpu.VMEM((rows, channels), bf16),
            pltpu.VMEM((rows, channels), bf16),
            pltpu.VMEM((rows, channels), bf16),
            pltpu.VMEM((tiles, REACH, TILE), bf16),
            pltpu.VMEM((tiles, REACH, TILE), bf16),
            pltpu.VMEM((2, Z, 2, 16, channels), bf16),
            pltpu.VMEM((6, 256, TILE), f32),
            pltpu.VMEM((4, 256, TILE), f32),
            pltpu.VMEM((tiles, 5, 256, TILE), f32),
            pltpu.VMEM((2, 256, TILE), f32),
            pltpu.VMEM((4, 768, TILE), bf16),
            pltpu.VMEM((2, 768, TILE), bf16),
            pltpu.VMEM((tiles, 2, 2, 2, 32, TILE), f32),
            pltpu.VMEM((tiles, 2, 2, 32, TILE), f32),
            pltpu.VMEM((tiles, 2, 32, TILE), f32),
            pltpu.VMEM((tiles, 32, TILE), f32),
            pltpu.VMEM((tiles, Z - 1, 8, TILE), f32),
            pltpu.VMEM((16, channels), f32),
            dma((5,)), dma((tiles,)),
            dma((2, tiles)), dma((2, tiles)),
            dma((3,)), dma((3,)), dma((3,)), dma((3,)), dma, dma,
            dma((tiles,)), dma((tiles,)),
            dma((tiles,)), dma((tiles,)),
            dma((tiles,)), dma((tiles,)),
            dma((tiles, 3)), dma((tiles, 3)),
            dma((tiles,)), dma((tiles,)),
        ],
        compiler_params=pltpu.CompilerParams(
            collective_id=0, has_side_effects=True, vmem_limit_bytes=56 << 20),
    )(counts, jnp.asarray(ana), jnp.asarray(syn), jnp.asarray(tsyn), x, g, taps)


def local(saved_input, out_grad, filter_taps, valid_counts):
    return fused(valid_counts, saved_input, out_grad, filter_taps)


def solution(mesh):
    return jax.shard_map(
        local,
        mesh=mesh,
        in_specs=(P("rep", "ctx", "ch"), P("rep", "ctx", "ch"), P("ctx", "ch"), P("rep", "ctx")),
        out_specs=(P("rep", "ctx", "ch"), P("ctx", "ch")),
        check_vma=False,
    )
```

```python
import functools
import math

import jax
import jax.numpy as jnp
import numpy as np
from jax import lax
from jax.experimental import pallas as pl
from jax.experimental.pallas import tpu as pltpu
from jax.sharding import PartitionSpec as P

REACH = 128
TILE = 256
STEP = 16
Z = 4


def transform_tables():
    freq = 2 * np.arange(128)[:, None] + 1
    analysis, synthesis = [], []
    for b in range(4):
        angle = np.pi * (freq * (np.arange(128)[None, :] + 128 * b) % 512) / 256.0
        forward = np.concatenate([np.cos(angle), -np.sin(angle)], 0)
        high = forward.astype(jnp.bfloat16)
        low = (forward - high.astype(np.float64)).astype(jnp.bfloat16)
        analysis.append(np.concatenate([high, low], 1))
        back = [part.astype(np.float64).T / 128 for part in (high, high, low)]
        synthesis.append(np.concatenate(back, 1))
    rows = [32 * z + 16 * core + r for core in range(2) for z in range(Z) for r in range(16)]
    tap_scale = 1.0 / 128
    taps = [synthesis[h][rows] * tap_scale for h in range(2)]
    return (np.stack(analysis), np.stack(synthesis).astype(jnp.bfloat16),
            np.stack(taps).astype(jnp.bfloat16))


def split(value):
    high = value.astype(jnp.bfloat16)
    low = (value - high.astype(jnp.float32)).astype(jnp.bfloat16)
    return high, low


def kernel(tiles, count_ref, ana_hbm, syn_hbm, tsyn_hbm, x_hbm, g_hbm, w_hbm,
           out_hbm, tap_hbm,
           ana_ref, syn_ref, tsyn_ref, gbuf, xbuf, obuf, from_left, from_right, wbuf,
           af, xf, wf, yf, tf, tap, pair_in, z_in, x_in, fin,
           load_sem, out_sem, halo_s, halo_r, wz_s, wz_r, wx_s, wx_r, wp_s, wp_r,
           p_s, p_r, z_s, z_r, x_s, x_r):
    live_count = count_ref[0, 0]
    ctx = lax.axis_index("ctx")
    rep = lax.axis_index("rep")
    ends = 16
    core = lax.rem(ctx, 2)
    z = lax.rem(lax.div(ctx, 2), Z)
    xlo = lax.div(ctx, 8)
    chunks = tiles // 2
    half_cols = chunks * TILE

    def device(x_lo, z_at, core_at, rep_at):
        return {"ctx": x_lo * 8 + z_at * 2 + core_at, "rep": rep_at}

    def remote(src, dst, send, recv, target):
        return pltpu.make_async_remote_copy(
            src_ref=src, dst_ref=dst, send_sem=send, recv_sem=recv,
            device_id=target, device_id_type=pl.DeviceIdType.MESH)

    left = {"ctx": lax.rem(ctx + ends - 1, ends), "rep": rep}
    right = {"ctx": lax.rem(ctx + 1, ends), "rep": rep}
    sibling = device(xlo, z, 1 - core, rep)
    x_near = device(1 - xlo, z, core, rep)
    x_wrap = device(1 - xlo, z, core, 1 - rep)
    x_far = device(xlo, z, core, 1 - rep)
    x_peers = (x_near, x_wrap, x_far)
    z_peers = [device(xlo, lax.rem(z + d, Z), core, rep) for d in range(1, Z)]

    barrier = pltpu.get_barrier_semaphore()
    peers = [left, right, x_near, x_wrap, x_far] + z_peers
    for peer in peers:
        pl.semaphore_signal(barrier, inc=1, device_id=peer, device_id_type=pl.DeviceIdType.MESH)

    own_half = pl.ds(pl.multiple_of(rep * half_cols, TILE // 2), half_cols)
    loads = [
        pltpu.make_async_copy(g_hbm.at[0, pl.ds(384, 128), :], gbuf.at[pl.ds(384, 128), :], load_sem.at[0]),
        pltpu.make_async_copy(w_hbm.at[:, own_half], wbuf.at[xlo, z, core, :, own_half], load_sem.at[1]),
        pltpu.make_async_copy(g_hbm.at[0, pl.ds(0, 384), :], gbuf.at[pl.ds(0, 384), :], load_sem.at[2]),
        pltpu.make_async_copy(x_hbm.at[0], xbuf, load_sem.at[3]),
        pltpu.make_async_copy(ana_hbm, ana_ref, load_sem.at[4]),
        pltpu.make_async_copy(tsyn_hbm, tsyn_ref, load_sem.at[5]),
        pltpu.make_async_copy(syn_hbm, syn_ref, load_sem.at[6]),
    ]
    for copy in loads:
        copy.start()

    def cols(i):
        return pl.ds(pl.multiple_of(i * TILE, TILE), TILE)

    def live_rows(b):
        rows = lax.broadcasted_iota(jnp.int32, (REACH, TILE), 0) + b * REACH
        return rows < live_count

    def halo_right(i):
        return remote(gbuf.at[pl.ds(384, 128), cols(i)], from_left.at[i],
                      halo_s.at[0, i], halo_r.at[0, i], right)

    def halo_left(i):
        return remote(g_hbm.at[0, pl.ds(0, 128), cols(i)], from_right.at[i],
                      halo_s.at[1, i], halo_r.at[1, i], left)

    def taps_z(d):
        return remote(w_hbm.at[:, own_half], wbuf.at[xlo, z, core, :, own_half],
                      wz_s.at[d], wz_r.at[d], z_peers[d])

    def taps_z_arrival(d):
        source = lax.rem(z + Z - 1 - d, Z)
        return remote(w_hbm.at[:, own_half], wbuf.at[xlo, source, core, :, own_half],
                      wz_s.at[d], wz_r.at[d], z_peers[d])

    def half_tile(half, c):
        return pl.ds(pl.multiple_of((half * chunks + c) * TILE, TILE), TILE)

    def taps_x(c, d):
        part = wbuf.at[xlo, :, core, :, half_tile(rep, c)]
        return remote(part, part, wx_s.at[c, d], wx_r.at[c, d], x_peers[d])

    def taps_x_arrival(c, d):
        x_from = (1 - xlo, 1 - xlo, xlo)[d]
        half_from = (rep, 1 - rep, 1 - rep)[d]
        part = wbuf.at[x_from, :, core, :, half_tile(half_from, c)]
        return remote(part, part, wx_s.at[c, d], wx_r.at[c, d], x_peers[d])

    def taps_pair(c, half, which):
        part = wbuf.at[:, :, which, :, half_tile(half, c)]
        return remote(part, part, wp_s.at[c, half], wp_r.at[c, half], sibling)

    def taps_forward(c):
        for d in range(3):
            taps_x_arrival(c, d).wait_recv()
        for half in range(2):
            taps_pair(c, half, core).start()

    def pair_copy(i):
        return remote(tap.at[i, 1 - core], pair_in.at[i], p_s.at[i], p_r.at[i], sibling)

    def z_copy(i, d):
        return remote(tap.at[i, core, lax.rem(z + 1 + d, Z)], z_in.at[i, d],
                      z_s.at[i, d], z_r.at[i, d], z_peers[d])

    def x_copy(i, d):
        h = (1 - xlo, 1 - xlo, xlo)[d]
        return remote(tap.at[i, core, z, h], x_in.at[i, d], x_s.at[i, d], x_r.at[i, d], x_peers[d])

    def stage_pair(i):
        pair_copy(i).wait_recv()
        tap[i, core] += pair_in[i]
        for d in range(Z - 1):
            z_copy(i, d).start()

    def stage_z(i):
        for d in range(Z - 1):
            z_copy(i, d).wait_recv()
        tap[i, core, z] = (tap[i, core, z] + z_in[i, 0]) + (z_in[i, 1] + z_in[i, 2])
        for d in range(3):
            x_copy(i, d).start()

    def stage_x(i):
        for d in range(3):
            x_copy(i, d).wait_recv()
        fin[:, cols(i)] = (tap[i, core, z, xlo] + x_in[i, 2]) + (x_in[i, 0] + x_in[i, 1])

    loads[0].wait()
    tail_live = live_rows(3)

    def mask_tail(i, carry):
        gbuf[pl.ds(384, 128), cols(i)] = jnp.where(tail_live, gbuf[pl.ds(384, 128), cols(i)], 0)
        return carry

    lax.fori_loop(0, tiles, mask_tail, None)
    pl.semaphore_wait(barrier, len(peers))

    def send_halo(i, carry):
        @pl.when(ctx < ends - 1)
        def _():
            halo_right(i).start()

        @pl.when(ctx > 0)
        def _():
            halo_left(i).start()

        return carry

    send_halo(0, None)
    for d in range(Z - 1):
        taps_z(d).start()
    lax.fori_loop(1, tiles, send_halo, None)

    @pl.when(ctx == 0)
    def _():
        from_left[...] = jnp.zeros_like(from_left)

    @pl.when(ctx == ends - 1)
    def _():
        from_right[...] = jnp.zeros_like(from_right)

    for copy in loads[2:5]:
        copy.wait()

    def analyse(b, block):
        return jnp.dot(ana_ref[b % 4], jnp.concatenate([block, block], 0),
                       preferred_element_type=jnp.float32)

    def put(ref, at, row, value):
        high, low = split(value)
        ref[at, pl.ds(row, STEP), :] = high
        ref[at, pl.ds(256 + row, STEP), :] = low
        ref[at, pl.ds(512 + row, STEP), :] = high

    def own_tile(i, carry):
        for b in range(4):
            rows = pl.ds(b * REACH, REACH)
            g_block, x_block = gbuf[rows, cols(i)], xbuf[rows, cols(i)]
            if b > 0:
                x_block = jnp.where(live_rows(b), x_block, 0)
            if b in (1, 2):
                g_block = jnp.where(live_rows(b), g_block, 0)
            af[i, b + 1] = analyse(b + 1, g_block)
            xf[i, b] = analyse(b, x_block)
        return carry

    lax.fori_loop(0, tiles, own_tile, None)
    loads[1].wait()
    for d in range(Z - 1):
        taps_z_arrival(d).wait_recv()
    for c in range(chunks):
        for d in range(3):
            taps_x(c, d).start()
    loads[5].wait()
    loads[6].wait()

    def windows(i, re, im):
        ar = [af[i, b, re, :] for b in range(6)]
        ai = [af[i, b, im, :] for b in range(6)]
        return [ar[b] + ar[b + 1] for b in range(5)], [ai[b] + ai[b + 1] for b in range(5)]

    def tap_tile(i, carry):
        @pl.when(ctx > 0)
        def _():
            halo_right(i).wait_recv()

        @pl.when(ctx < ends - 1)
        def _():
            halo_left(i).wait_recv()

        af[i, 0] = analyse(0, from_left[i])
        af[i, 5] = analyse(5, from_right[i])

        def chunk(c, carry):
            row = pl.multiple_of(c * STEP, STEP)
            re, im = pl.ds(row, STEP), pl.ds(128 + row, STEP)
            gr, gi = windows(i, re, im)
            for h in range(2):
                tr = ti = None
                for b in range(4):
                    xr, xi = xf[i, b, re, :], xf[i, b, im, :]
                    pr = xr * gr[b + h] + xi * gi[b + h]
                    pi = xr * gi[b + h] - xi * gr[b + h]
                    tr, ti = (pr, pi) if tr is None else (tr + pr, ti + pi)
                put(tf, h, row, tr)
                put(tf, h, 128 + row, ti)
            return carry

        lax.fori_loop(0, 128 // STEP, chunk, None, unroll=True)
        for h in range(2):
            terms = jnp.dot(tsyn_ref[h], tf[h], preferred_element_type=jnp.float32)
            for core_at in range(2):
                for z_at in range(Z):
                    start = (core_at * Z + z_at) * 16
                    tap[i, core_at, z_at, h] = terms[start:start + 16]
        pair_copy(i).start()

        @pl.when(i >= 1)
        def _():
            stage_pair(i - 1)

        for c in range(min(2, chunks)):
            @pl.when(i == tiles - 2 + c)
            def _(c=c):
                taps_forward(c)

        return carry

    lax.fori_loop(0, tiles, tap_tile, None)
    stage_pair(tiles - 1)

    def store_out(i):
        return pltpu.make_async_copy(obuf.at[:, cols(i)], out_hbm.at[0, :, cols(i)], out_sem.at[i])

    def grad_tile(k, carry):
        chunk_at = lax.div(k, 2)
        i = lax.rem(k, 2) * chunks + chunk_at

        @pl.when(lax.rem(k, 2) == 0)
        def _():
            for half in range(2):
                taps_pair(chunk_at, half, 1 - core).wait_recv()

        for h in range(2):
            block = wbuf[h, :, :, :, cols(i)].reshape(REACH, TILE)
            wf[h] = analyse(h, block)

        def chunk(c, carry):
            row = pl.multiple_of(c * STEP, STEP)
            re, im = pl.ds(row, STEP), pl.ds(128 + row, STEP)
            gr, gi = windows(i, re, im)
            w0r, w0i = wf[0, re, :], wf[0, im, :]
            w1r, w1i = wf[1, re, :], wf[1, im, :]
            for b in range(4):
                yr = (w0r * gr[b] + w0i * gi[b]) + (w1r * gr[b + 1] + w1i * gi[b + 1])
                yi = (w0r * gi[b] - w0i * gr[b]) + (w1r * gi[b + 1] - w1i * gr[b + 1])
                put(yf, b, row, yr)
                put(yf, b, 128 + row, yi)
            return carry

        lax.fori_loop(0, 128 // STEP, chunk, None, unroll=True)
        for b in range(4):
            value = jnp.dot(syn_ref[b], yf[b], preferred_element_type=jnp.float32)
            if b > 0:
                value = jnp.where(live_rows(b), value, 0)
            obuf[pl.ds(b * REACH, REACH), cols(i)] = value.astype(jnp.bfloat16)
        store_out(i).start()
        @pl.when(jnp.logical_and(lax.rem(k, 2) == 1, chunk_at + 2 < chunks))
        def _():
            taps_forward(chunk_at + 2)

        @pl.when(k >= 1)
        def _():
            stage_z(k - 1)

        return carry

    lax.fori_loop(0, tiles, grad_tile, None)
    stage_z(tiles - 1)

    def total(i, carry):
        stage_x(i)
        return carry

    lax.fori_loop(0, tiles, total, None)
    last = pltpu.make_async_copy(fin, tap_hbm, load_sem.at[7])
    last.start()

    def finish(i, carry):
        store_out(i).wait()
        pair_copy(i).wait_send()
        for d in range(3):
            z_copy(i, d).wait_send()
            x_copy(i, d).wait_send()

        @pl.when(ctx < ends - 1)
        def _():
            halo_right(i).wait_send()

        @pl.when(ctx > 0)
        def _():
            halo_left(i).wait_send()

        return carry

    lax.fori_loop(0, tiles, finish, None)
    for d in range(3):
        taps_z(d).wait_send()
    for c in range(chunks):
        for d in range(3):
            taps_x(c, d).wait_send()
        for half in range(2):
            taps_pair(c, half, core).wait_send()
    last.wait()


def fused(counts, x, g, taps):
    _, rows, channels = x.shape
    tiles = channels // TILE
    ana, syn, tsyn = transform_tables()
    dma = pltpu.SemaphoreType.DMA
    hbm = pl.BlockSpec(memory_space=pl.ANY)
    f32, bf16 = jnp.float32, jnp.bfloat16
    return pl.pallas_call(
        functools.partial(kernel, tiles),
        out_shape=(jax.ShapeDtypeStruct(x.shape, bf16),
                   jax.ShapeDtypeStruct(taps.shape, f32)),
        in_specs=[pl.BlockSpec(memory_space=pltpu.SMEM)] + [hbm] * 6,
        out_specs=(hbm, hbm),
        scratch_shapes=[
            pltpu.VMEM(ana.shape, bf16),
            pltpu.VMEM(syn.shape, bf16),
            pltpu.VMEM(tsyn.shape, bf16),
            pltpu.VMEM((rows, channels), bf16),
            pltpu.VMEM((rows, channels), bf16),
            pltpu.VMEM((rows, channels), bf16),
            pltpu.VMEM((tiles, REACH, TILE), bf16),
            pltpu.VMEM((tiles, REACH, TILE), bf16),
            pltpu.VMEM((2, Z, 2, 16, channels), bf16),
            pltpu.VMEM((tiles, 6, 256, TILE), f32),
            pltpu.VMEM((tiles, 4, 256, TILE), f32),
            pltpu.VMEM((2, 256, TILE), f32),
            pltpu.VMEM((4, 768, TILE), bf16),
            pltpu.VMEM((2, 768, TILE), bf16),
            pltpu.VMEM((tiles, 2, Z, 2, 16, TILE), f32),
            pltpu.VMEM((tiles, Z, 2, 16, TILE), f32),
            pltpu.VMEM((tiles, 3, 2, 16, TILE), f32),
            pltpu.VMEM((tiles, 3, 16, TILE), f32),
            pltpu.VMEM((16, channels), f32),
            dma((8,)), dma((tiles,)),
            dma((2, tiles)), dma((2, tiles)),
            dma((3,)), dma((3,)),
            dma((tiles // 2, 3)), dma((tiles // 2, 3)),
            dma((tiles // 2, 2)), dma((tiles // 2, 2)),
            dma((tiles,)), dma((tiles,)),
            dma((tiles, 3)), dma((tiles, 3)),
            dma((tiles, 3)), dma((tiles, 3)),
        ],
        compiler_params=pltpu.CompilerParams(
            collective_id=0, has_side_effects=True, vmem_limit_bytes=56 << 20),
    )(counts, jnp.asarray(ana), jnp.asarray(syn), jnp.asarray(tsyn), x, g, taps)


def local(saved_input, out_grad, filter_taps, valid_counts):
    return fused(valid_counts, saved_input, out_grad, filter_taps)


def solution(mesh):
    return jax.shard_map(
        local,
        mesh=mesh,
        in_specs=(P("rep", "ctx", "ch"), P("rep", "ctx", "ch"), P("ctx", "ch"), P("rep", "ctx")),
        out_specs=(P("rep", "ctx", "ch"), P("ctx", "ch")),
        check_vma=False,
    )
```

```python
import functools
import math

import jax
import jax.numpy as jnp
import numpy as np
from jax import lax
from jax.experimental import pallas as pl
from jax.experimental.pallas import tpu as pltpu
from jax.sharding import PartitionSpec as P

REACH = 128
TILE = 256
STEP = 16
Z = 4


def transform_tables():
    freq = 2 * np.arange(128)[:, None] + 1
    analysis, synthesis = [], []
    for b in range(4):
        angle = np.pi * (freq * (np.arange(128)[None, :] + 128 * b) % 512) / 256.0
        forward = np.concatenate([np.cos(angle), -np.sin(angle)], 0)
        high = forward.astype(jnp.bfloat16)
        low = (forward - high.astype(np.float64)).astype(jnp.bfloat16)
        analysis.append(np.concatenate([high, low], 1))
        back = [part.astype(np.float64).T / 128 for part in (high, high, low)]
        synthesis.append(np.concatenate(back, 1))
    x_rows = [32 * z + 16 * core + 8 * half + r
              for core in range(2) for half in range(2) for z in range(Z) for r in range(8)]
    z_rows = [32 * z + 16 * core + r for core in range(2) for z in range(Z) for r in range(16)]
    tap_scale = 1.0 / 128
    taps = np.stack([np.stack([synthesis[h][rows] * tap_scale for h in range(2)])
                     for rows in (x_rows, z_rows)])
    return (np.stack(analysis), np.stack(synthesis).astype(jnp.bfloat16), taps.astype(jnp.bfloat16))


def split(value):
    high = value.astype(jnp.bfloat16)
    low = (value - high.astype(jnp.float32)).astype(jnp.bfloat16)
    return high, low


def kernel(tiles, count_ref, ana_hbm, syn_hbm, tsyn_hbm, x_hbm, g_hbm, w_hbm,
           out_ref, tap_out,
           ana_ref, syn_ref, tsyn_ref, live_ref, gbuf, xbuf, from_left, from_right, wbuf,
           af, xf, wf, ya, yb, tf, tap, pair_in, q_in, e_in, z_in, x_in, fin,
           load_sem, halo_s, halo_r, wz_s, wz_r, wx_s, wx_r, wp_s, wp_r,
           p_s, p_r, q_s, q_r, e_s, e_r, h_s, h_r, z_s, z_r, x_s, x_r):
    live_count = count_ref[0, 0]
    ctx = lax.axis_index("ctx")
    rep = lax.axis_index("rep")
    ends = 16
    core = lax.rem(ctx, 2)
    z = lax.rem(lax.div(ctx, 2), Z)
    xlo = lax.div(ctx, 8)
    chunks = tiles // 2
    half_cols = chunks * TILE
    x_first = tiles // 2

    def device(x_lo, z_at, core_at, rep_at):
        return {"ctx": x_lo * 8 + z_at * 2 + core_at, "rep": rep_at}

    def remote(src, dst, send, recv, target):
        return pltpu.make_async_remote_copy(
            src_ref=src, dst_ref=dst, send_sem=send, recv_sem=recv,
            device_id=target, device_id_type=pl.DeviceIdType.MESH)

    left = {"ctx": lax.rem(ctx + ends - 1, ends), "rep": rep}
    right = {"ctx": lax.rem(ctx + 1, ends), "rep": rep}
    sibling = device(xlo, z, 1 - core, rep)
    x_near = device(1 - xlo, z, core, rep)
    x_wrap = device(1 - xlo, z, core, 1 - rep)
    x_far = device(xlo, z, core, 1 - rep)
    x_peers = (x_near, x_wrap, x_far)
    z_peers = [device(xlo, lax.rem(z + d, Z), core, rep) for d in range(1, Z)]

    barrier = pltpu.get_barrier_semaphore()
    peers = [left, right, x_near, x_wrap, x_far] + z_peers
    for peer in peers:
        pl.semaphore_signal(barrier, inc=1, device_id=peer, device_id_type=pl.DeviceIdType.MESH)

    own_half = pl.ds(pl.multiple_of(rep * half_cols, TILE // 2), half_cols)
    loads = [
        pltpu.make_async_copy(g_hbm.at[0, pl.ds(384, 128), :], gbuf.at[pl.ds(384, 128), :], load_sem.at[0]),
        pltpu.make_async_copy(w_hbm.at[:, own_half], wbuf.at[xlo, z, core, :, own_half], load_sem.at[1]),
        pltpu.make_async_copy(g_hbm.at[0, pl.ds(0, 384), :], gbuf.at[pl.ds(0, 384), :], load_sem.at[2]),
        pltpu.make_async_copy(x_hbm.at[0], xbuf, load_sem.at[3]),
        pltpu.make_async_copy(ana_hbm, ana_ref, load_sem.at[4]),
        pltpu.make_async_copy(tsyn_hbm, tsyn_ref, load_sem.at[5]),
        pltpu.make_async_copy(syn_hbm, syn_ref, load_sem.at[6]),
    ]
    for copy in loads:
        copy.start()

    def cols(i):
        return pl.ds(pl.multiple_of(i * TILE, TILE), TILE)

    def halo_right(i):
        return remote(gbuf.at[pl.ds(384, 128), cols(i)], from_left.at[i],
                      halo_s.at[0, i], halo_r.at[0, i], right)

    def halo_left(i):
        return remote(g_hbm.at[0, pl.ds(0, 128), cols(i)], from_right.at[i],
                      halo_s.at[1, i], halo_r.at[1, i], left)

    def taps_z(d):
        return remote(w_hbm.at[:, own_half], wbuf.at[xlo, z, core, :, own_half],
                      wz_s.at[d], wz_r.at[d], z_peers[d])

    def taps_z_arrival(d):
        source = lax.rem(z + Z - 1 - d, Z)
        return remote(w_hbm.at[:, own_half], wbuf.at[xlo, source, core, :, own_half],
                      wz_s.at[d], wz_r.at[d], z_peers[d])

    def half_tile(half, c):
        return pl.ds(pl.multiple_of((half * chunks + c) * TILE, TILE), TILE)

    def taps_x(c, d):
        part = wbuf.at[xlo, :, core, :, half_tile(rep, c)]
        return remote(part, part, wx_s.at[c, d], wx_r.at[c, d], x_peers[d])

    def taps_x_arrival(c, d):
        x_from = (1 - xlo, 1 - xlo, xlo)[d]
        half_from = (rep, 1 - rep, 1 - rep)[d]
        part = wbuf.at[x_from, :, core, :, half_tile(half_from, c)]
        return remote(part, part, wx_s.at[c, d], wx_r.at[c, d], x_peers[d])

    def taps_pair(c, half, which):
        part = wbuf.at[:, :, which, :, half_tile(half, c)]
        return remote(part, part, wp_s.at[c, half], wp_r.at[c, half], sibling)

    def taps_forward(c):
        for d in range(3):
            taps_x_arrival(c, d).wait_recv()
        for half in range(2):
            taps_pair(c, half, core).start()

    def pair_copy(i):
        return remote(tap.at[i, 1 - core], pair_in.at[i], p_s.at[i], p_r.at[i], sibling)

    def quarter_copy(i, d):
        h = (1 - xlo, 1 - xlo, xlo)[d]
        half = (rep, 1 - rep, 1 - rep)[d]
        return remote(tap.at[i, core, pl.ds((h * 2 + half) * 2, 2)], q_in.at[i, d],
                      q_s.at[i, d], q_r.at[i, d], x_peers[d])

    def eighth(i, z_at):
        rows = pl.ds(pl.multiple_of(lax.rem(z_at, 2) * 8, 8), 8)
        return tap.at[i, core, (xlo * 2 + rep) * 2 + lax.div(z_at, 2), rows]

    def eighth_copy(i, d):
        return remote(eighth(i, lax.rem(z + 1 + d, Z)), e_in.at[i, d],
                      e_s.at[i, d], e_r.at[i, d], z_peers[d])

    def swap_copy(i, which):
        part = fin.at[pl.ds(pl.multiple_of(which * 8, 8), 8), cols(i)]
        return remote(part, part, h_s.at[i], h_r.at[i], x_far)

    def stage_quarter(i):
        for d in range(3):
            quarter_copy(i, d).wait_recv()
        mine = pl.ds((xlo * 2 + rep) * 2, 2)
        tap[i, core, mine] = (tap[i, core, mine] + q_in[i, 0]) + (q_in[i, 1] + q_in[i, 2])
        for d in range(Z - 1):
            eighth_copy(i, d).start()

    def stage_eighth(i):
        for d in range(Z - 1):
            eighth_copy(i, d).wait_recv()
        total = (eighth(i, z)[...] + e_in[i, 0]) + (e_in[i, 1] + e_in[i, 2])
        fin[pl.ds(pl.multiple_of(rep * 8, 8), 8), cols(i)] = total
        swap_copy(i, rep).start()

    def z_copy(i, d):
        piece = pl.ds(lax.rem(z + 1 + d, Z) * 2, 2)
        at = i - x_first
        return remote(tap.at[i, core, piece], z_in.at[at, d], z_s.at[at, d], z_r.at[at, d], z_peers[d])

    def x_copy(i, d):
        h = (1 - xlo, 1 - xlo, xlo)[d]
        at = i - x_first
        return remote(tap.at[i, core, z * 2 + h], x_in.at[at, d], x_s.at[at, d], x_r.at[at, d], x_peers[d])

    def stage_pair(i):
        pair_copy(i).wait_recv()
        tap[i, core] += pair_in[i]

        @pl.when(i < x_first)
        def _():
            for d in range(3):
                quarter_copy(i, d).start()

        @pl.when(i >= x_first)
        def _():
            for d in range(Z - 1):
                z_copy(i, d).start()

    def stage_z(i):
        at = i - x_first
        for d in range(Z - 1):
            z_copy(i, d).wait_recv()
        mine = pl.ds(z * 2, 2)
        tap[i, core, mine] = (tap[i, core, mine] + z_in[at, 0]) + (z_in[at, 1] + z_in[at, 2])
        for d in range(3):
            x_copy(i, d).start()

    def stage_x(i):
        at = i - x_first
        for d in range(3):
            x_copy(i, d).wait_recv()
        fin[:, cols(i)] = (tap[i, core, z * 2 + xlo] + x_in[at, 2]) + (x_in[at, 0] + x_in[at, 1])

    for b in range(4):
        rows = lax.broadcasted_iota(jnp.int32, (REACH, TILE), 0) + b * REACH
        live_ref[pl.ds(b * REACH, REACH), :] = jnp.where(rows < live_count, 1.0, 0.0).astype(jnp.bfloat16)
    loads[0].wait()

    def mask_tail(i, carry):
        gbuf[pl.ds(384, 128), cols(i)] = gbuf[pl.ds(384, 128), cols(i)] * live_ref[pl.ds(384, 128), :]
        return carry

    lax.fori_loop(0, tiles, mask_tail, None)
    pl.semaphore_wait(barrier, len(peers))

    def send_halo(i, carry):
        @pl.when(ctx < ends - 1)
        def _():
            halo_right(i).start()

        @pl.when(ctx > 0)
        def _():
            halo_left(i).start()

        return carry

    send_halo(0, None)
    for d in range(Z - 1):
        taps_z(d).start()
    lax.fori_loop(1, tiles, send_halo, None)

    @pl.when(ctx == 0)
    def _():
        from_left[...] = jnp.zeros_like(from_left)

    @pl.when(ctx == ends - 1)
    def _():
        from_right[...] = jnp.zeros_like(from_right)

    for copy in loads[2:5]:
        copy.wait()

    def analyse(b, block):
        return jnp.dot(ana_ref[b % 4], jnp.concatenate([block, block], 0),
                       preferred_element_type=jnp.float32)

    def put(ref, at, row, value):
        high, low = split(value)
        ref[at, pl.ds(row, STEP), :] = high
        ref[at, pl.ds(256 + row, STEP), :] = low

    def synthesise(table, spectrum, at):
        terms = jnp.concatenate([spectrum[at], spectrum[at, pl.ds(0, 256), :]], 0)
        return jnp.dot(table, terms, preferred_element_type=jnp.float32)

    def own_tile(i, carry):
        for b in range(4):
            rows = pl.ds(b * REACH, REACH)
            g_block, x_block = gbuf[rows, cols(i)], xbuf[rows, cols(i)]
            if b > 0:
                x_block = x_block * live_ref[rows, :]
            if b in (1, 2):
                g_block = g_block * live_ref[rows, :]
            af[i, b + 1] = analyse(b + 1, g_block)
            xf[i, b] = analyse(b, x_block)
        return carry

    lax.fori_loop(0, tiles, own_tile, None)
    loads[1].wait()
    for d in range(Z - 1):
        taps_z_arrival(d).wait_recv()
    for c in range(chunks):
        for d in range(3):
            taps_x(c, d).start()
    loads[5].wait()
    loads[6].wait()

    def windows(i, re, im):
        ar = [af[i, b, re, :] for b in range(6)]
        ai = [af[i, b, im, :] for b in range(6)]
        return [ar[b] + ar[b + 1] for b in range(5)], [ai[b] + ai[b + 1] for b in range(5)]

    def tap_tile(i, carry):
        @pl.when(ctx > 0)
        def _():
            halo_right(i).wait_recv()

        @pl.when(ctx < ends - 1)
        def _():
            halo_left(i).wait_recv()

        af[i, 0] = analyse(0, from_left[i])
        af[i, 5] = analyse(5, from_right[i])

        def chunk(c, carry):
            row = pl.multiple_of(c * STEP, STEP)
            re, im = pl.ds(row, STEP), pl.ds(128 + row, STEP)
            gr, gi = windows(i, re, im)
            for h in range(2):
                tr = ti = None
                for b in range(4):
                    xr, xi = xf[i, b, re, :], xf[i, b, im, :]
                    pr = xr * gr[b + h] + xi * gi[b + h]
                    pi = xr * gi[b + h] - xi * gr[b + h]
                    tr, ti = (pr, pi) if tr is None else (tr + pr, ti + pi)
                put(tf, h, row, tr)
                put(tf, h, 128 + row, ti)
            return carry

        lax.fori_loop(0, 128 // STEP, chunk, None, unroll=True)
        for h in range(2):
            kind = jnp.where(i < x_first, 0, 1)
            terms = synthesise(tsyn_ref[kind, h], tf, h)
            for core_at in range(2):
                for u in range(4):
                    start = core_at * 64 + u * 16
                    unit = jnp.where(i < x_first, h * 4 + u, u * 2 + h)
                    tap[i, core_at, unit] = terms[start:start + 16]
        pair_copy(i).start()

        @pl.when(i >= 1)
        def _():
            stage_pair(i - 1)

        @pl.when(i == tiles - 1)
        def _():
            taps_forward(0)

        return carry

    lax.fori_loop(0, tiles, tap_tile, None)
    stage_pair(tiles - 1)
    if chunks > 1:
        taps_forward(1)

    def weigh(i, at, spectrum):
        def chunk(c, carry):
            row = pl.multiple_of(c * STEP, STEP)
            re, im = pl.ds(row, STEP), pl.ds(128 + row, STEP)
            gr, gi = windows(i, re, im)
            w0r, w0i = wf[at, re, :], wf[at, im, :]
            w1r, w1i = wf[at + 1, re, :], wf[at + 1, im, :]
            for b in range(4):
                yr = (w0r * gr[b] + w0i * gi[b]) + (w1r * gr[b + 1] + w1i * gi[b + 1])
                yi = (w0r * gi[b] - w0i * gr[b]) + (w1r * gi[b + 1] - w1i * gr[b + 1])
                put(spectrum, b, row, yr)
                put(spectrum, b, 128 + row, yi)
            return carry

        lax.fori_loop(0, 128 // STEP, chunk, None, unroll=True)

    def emit(i, spectrum):
        for b in range(4):
            rows = pl.ds(b * REACH, REACH)
            value = synthesise(syn_ref[b], spectrum, b).astype(jnp.bfloat16)
            if b > 0:
                value = value * live_ref[rows, :]
            out_ref[0, rows, cols(i)] = value

    def grad_tiles(c, carry):
        for half in range(2):
            taps_pair(c, half, 1 - core).wait_recv()
        first, second = c, chunks + c
        for half, i in ((0, first), (1, second)):
            for h in range(2):
                block = wbuf[h, :, :, :, cols(i)].reshape(REACH, TILE)
                wf[half * 2 + h] = analyse(h, block)
        weigh(first, 0, ya)
        weigh(second, 2, yb)
        emit(first, ya)
        emit(second, yb)

        @pl.when(c + 2 < chunks)
        def _():
            taps_forward(c + 2)

        @pl.when(c < 2)
        def _():
            for part in range(x_first // 2):
                stage_quarter(c * (x_first // 2) + part)

        @pl.when(c >= 2)
        def _():
            for part in range(x_first // 2):
                stage_eighth((c - 2) * (x_first // 2) + part)

        @pl.when(c >= 1)
        def _():
            stage_z(x_first + c - 1)

        return carry

    lax.fori_loop(0, chunks, grad_tiles, None)
    stage_z(tiles - 1)
    for i in range(x_first):
        stage_x(x_first + i)
        swap_copy(i, 1 - rep).wait_recv()
    tap_out[...] = fin[...]

    def finish(i, carry):
        pair_copy(i).wait_send()

        @pl.when(i < x_first)
        def _():
            for d in range(3):
                quarter_copy(i, d).wait_send()
                eighth_copy(i, d).wait_send()
            swap_copy(i, rep).wait_send()

        @pl.when(i >= x_first)
        def _():
            for d in range(3):
                z_copy(i, d).wait_send()
                x_copy(i, d).wait_send()

        @pl.when(ctx < ends - 1)
        def _():
            halo_right(i).wait_send()

        @pl.when(ctx > 0)
        def _():
            halo_left(i).wait_send()

        return carry

    lax.fori_loop(0, tiles, finish, None)
    for d in range(3):
        taps_z(d).wait_send()
    for c in range(chunks):
        for d in range(3):
            taps_x(c, d).wait_send()
        for half in range(2):
            taps_pair(c, half, core).wait_send()


def fused(counts, x, g, taps):
    _, rows, channels = x.shape
    tiles = channels // TILE
    ana, syn, tsyn = transform_tables()
    dma = pltpu.SemaphoreType.DMA
    hbm = pl.BlockSpec(memory_space=pl.ANY)
    f32, bf16 = jnp.float32, jnp.bfloat16
    vmem = pl.BlockSpec(memory_space=pltpu.VMEM)
    first, rest = tiles // 2, tiles - tiles // 2
    return pl.pallas_call(
        functools.partial(kernel, tiles),
        out_shape=(pltpu.VMEM(x.shape, bf16), pltpu.VMEM(taps.shape, f32)),
        in_specs=[pl.BlockSpec(memory_space=pltpu.SMEM)] + [hbm] * 6,
        out_specs=(vmem, vmem),
        scratch_shapes=[
            pltpu.VMEM(ana.shape, bf16),
            pltpu.VMEM(syn.shape, bf16),
            pltpu.VMEM(tsyn.shape, bf16),
            pltpu.VMEM((rows, TILE), bf16),
            pltpu.VMEM((rows, channels), bf16),
            pltpu.VMEM((rows, channels), bf16),
            pltpu.VMEM((tiles, REACH, TILE), bf16),
            pltpu.VMEM((tiles, REACH, TILE), bf16),
            pltpu.VMEM((2, Z, 2, 16, channels), bf16),
            pltpu.VMEM((tiles, 6, 256, TILE), f32),
            pltpu.VMEM((tiles, 4, 256, TILE), f32),
            pltpu.VMEM((4, 256, TILE), f32),
            pltpu.VMEM((4, 512, TILE), bf16),
            pltpu.VMEM((4, 512, TILE), bf16),
            pltpu.VMEM((2, 512, TILE), bf16),
            pltpu.VMEM((tiles, 2, 8, 16, TILE), f32),
            pltpu.VMEM((tiles, 8, 16, TILE), f32),
            pltpu.VMEM((first, 3, 2, 16, TILE), f32),
            pltpu.VMEM((first, 3, 8, TILE), f32),
            pltpu.VMEM((rest, 3, 2, 16, TILE), f32),
            pltpu.VMEM((rest, 3, 16, TILE), f32),
            pltpu.VMEM((16, channels), f32),
            dma((8,)),
            dma((2, tiles)), dma((2, tiles)),
            dma((3,)), dma((3,)),
            dma((tiles // 2, 3)), dma((tiles // 2, 3)),
            dma((tiles // 2, 2)), dma((tiles // 2, 2)),
            dma((tiles,)), dma((tiles,)),
            dma((first, 3)), dma((first, 3)),
            dma((first, 3)), dma((first, 3)),
            dma((first,)), dma((first,)),
            dma((rest, 3)), dma((rest, 3)),
            dma((rest, 3)), dma((rest, 3)),
        ],
        compiler_params=pltpu.CompilerParams(
            collective_id=0, has_side_effects=True, vmem_limit_bytes=56 << 20),
    )(counts, jnp.asarray(ana), jnp.asarray(syn), jnp.asarray(tsyn), x, g, taps)


def local(saved_input, out_grad, filter_taps, valid_counts):
    return fused(valid_counts, saved_input, out_grad, filter_taps)


def solution(mesh):
    return jax.shard_map(
        local,
        mesh=mesh,
        in_specs=(P("rep", "ctx", "ch"), P("rep", "ctx", "ch"), P("ctx", "ch"), P("rep", "ctx")),
        out_specs=(P("rep", "ctx", "ch"), P("ctx", "ch")),
        check_vma=False,
    )
```

```python
import functools
import math

import jax
import jax.numpy as jnp
import numpy as np
from jax import lax
from jax.experimental import pallas as pl
from jax.experimental.pallas import tpu as pltpu
from jax.sharding import PartitionSpec as P

REACH = 128
TILE = 256
STEP = 16
X_FIRST = 3
HALO_FROM = 2
Z = 4


def transform_tables():
    freq = 2 * np.arange(128)[:, None] + 1
    analysis, synthesis = [], []
    for b in range(4):
        angle = np.pi * (freq * (np.arange(128)[None, :] + 128 * b) % 512) / 256.0
        forward = np.concatenate([np.cos(angle), -np.sin(angle)], 0)
        high = forward.astype(jnp.bfloat16)
        low = (forward - high.astype(np.float64)).astype(jnp.bfloat16)
        analysis.append(np.concatenate([high, low], 1))
        back = [part.astype(np.float64).T / 128 for part in (high, high, low)]
        synthesis.append(np.concatenate(back, 1))
    x_rows = [32 * z + 16 * core + 8 * half + r
              for core in range(2) for half in range(2) for z in range(Z) for r in range(8)]
    z_rows = [32 * z + 16 * core + r for core in range(2) for z in range(Z) for r in range(16)]
    tap_scale = 1.0 / 128
    taps = np.stack([np.stack([synthesis[h][rows] * tap_scale for h in range(2)])
                     for rows in (x_rows, z_rows)])
    return (np.stack(analysis), np.stack(synthesis).astype(jnp.bfloat16), taps.astype(jnp.bfloat16))


def reduction_plan(tiles, x_first, chunks):
    early, late = list(range(x_first)), list(range(x_first, tiles))
    cut = (x_first + 1) // 2
    plan = [[("quarter", i) for i in early[:cut]] + [("z", i) for i in late[:1]],
            [("quarter", i) for i in early[cut:]] + [("z", i) for i in late[1:2]],
            [("eighth", i) for i in early[:cut]] + [("z", i) for i in late[2:3]],
            [("eighth", i) for i in early[cut:]] + [("z", i) for i in late[3:4]],
            [("z", i) for i in late[4:]] + [("x", i) for i in late] + [("swap", i) for i in early]]
    assert len(plan) == chunks + 1
    return plan


def split(value):
    high = value.astype(jnp.bfloat16)
    low = (value - high.astype(jnp.float32)).astype(jnp.bfloat16)
    return high, low


def kernel(tiles, count_ref, ana_hbm, syn_hbm, tsyn_hbm, x_hbm, g_hbm, w_hbm,
           out_ref, tap_out,
           ana_ref, syn_ref, tsyn_ref, live_ref, gbuf, xbuf, from_left, from_right, wbuf,
           af, xf, wf, ya, yb, tf, tap, pair_in, q_in, e_in, z_in, x_in, fin,
           load_sem, halo_s, halo_r, wz_s, wz_r, wx_s, wx_r, wp_s, wp_r,
           p_s, p_r, q_s, q_r, e_s, e_r, h_s, h_r, z_s, z_r, x_s, x_r):
    live_count = count_ref[0, 0]
    ctx = lax.axis_index("ctx")
    rep = lax.axis_index("rep")
    ends = 16
    core = lax.rem(ctx, 2)
    z = lax.rem(lax.div(ctx, 2), Z)
    xlo = lax.div(ctx, 8)
    chunks = tiles // 2
    x_first = X_FIRST

    def device(x_lo, z_at, core_at, rep_at):
        return {"ctx": x_lo * 8 + z_at * 2 + core_at, "rep": rep_at}

    def remote(src, dst, send, recv, target):
        return pltpu.make_async_remote_copy(
            src_ref=src, dst_ref=dst, send_sem=send, recv_sem=recv,
            device_id=target, device_id_type=pl.DeviceIdType.MESH)

    left = {"ctx": lax.rem(ctx + ends - 1, ends), "rep": rep}
    right = {"ctx": lax.rem(ctx + 1, ends), "rep": rep}
    sibling = device(xlo, z, 1 - core, rep)
    x_near = device(1 - xlo, z, core, rep)
    x_wrap = device(1 - xlo, z, core, 1 - rep)
    x_far = device(xlo, z, core, 1 - rep)
    x_peers = (x_near, x_wrap, x_far)
    z_peers = [device(xlo, lax.rem(z + d, Z), core, rep) for d in range(1, Z)]

    barrier = pltpu.get_barrier_semaphore()
    peers = [left, right, x_near, x_wrap, x_far] + z_peers
    for peer in peers:
        pl.semaphore_signal(barrier, inc=1, device_id=peer, device_id_type=pl.DeviceIdType.MESH)

    loads = [
        pltpu.make_async_copy(g_hbm.at[0, pl.ds(384, 128), :], gbuf.at[pl.ds(384, 128), :], load_sem.at[0]),
        pltpu.make_async_copy(w_hbm, wbuf.at[xlo, z, core], load_sem.at[1]),
        pltpu.make_async_copy(g_hbm.at[0, pl.ds(0, 384), :], gbuf.at[pl.ds(0, 384), :], load_sem.at[2]),
        pltpu.make_async_copy(x_hbm.at[0], xbuf, load_sem.at[3]),
        pltpu.make_async_copy(ana_hbm, ana_ref, load_sem.at[4]),
        pltpu.make_async_copy(tsyn_hbm, tsyn_ref, load_sem.at[5]),
        pltpu.make_async_copy(syn_hbm, syn_ref, load_sem.at[6]),
    ]
    for copy in loads:
        copy.start()

    def cols(i):
        return pl.ds(pl.multiple_of(i * TILE, TILE), TILE)

    def tile_at(slot):
        mixed = lax.rem(slot, 2) * x_first + lax.div(slot, 2)
        return jnp.where(slot < 2 * x_first, mixed, slot)

    def halo_right(i):
        return remote(gbuf.at[pl.ds(384, 128), cols(i)], from_left.at[i],
                      halo_s.at[0, i], halo_r.at[0, i], right)

    def halo_left(i):
        return remote(g_hbm.at[0, pl.ds(0, 128), cols(i)], from_right.at[i],
                      halo_s.at[1, i], halo_r.at[1, i], left)

    def pair_cols(c):
        return pl.ds(pl.multiple_of(c * 2 * TILE, 2 * TILE), 2 * TILE)

    def taps_z(c, d):
        return remote(w_hbm.at[:, pair_cols(c)], wbuf.at[xlo, z, core, :, pair_cols(c)],
                      wz_s.at[c, d], wz_r.at[c, d], z_peers[d])

    def taps_z_arrival(c, d):
        source = lax.rem(z + Z - 1 - d, Z)
        return remote(w_hbm.at[:, pair_cols(c)], wbuf.at[xlo, source, core, :, pair_cols(c)],
                      wz_s.at[c, d], wz_r.at[c, d], z_peers[d])

    def taps_x(c, d, which):
        part = wbuf.at[which, :, core, :, cols(2 * c + d)]
        return remote(part, part, wx_s.at[c, d], wx_r.at[c, d], x_peers[d])

    def taps_pair(c, which):
        part = wbuf.at[:, :, which, :, pair_cols(c)]
        return remote(part, part, wp_s.at[c], wp_r.at[c], sibling)

    def taps_to_x(c):
        for d in range(Z - 1):
            taps_z_arrival(c, d).wait_recv()
        for d in range(2):
            taps_x(c, d, xlo).start()

    def taps_to_pair(c):
        for d in range(2):
            taps_x(c, d, 1 - xlo).wait_recv()
        taps_pair(c, core).start()

    def pair_copy(i):
        return remote(tap.at[i, 1 - core], pair_in.at[i], p_s.at[i], p_r.at[i], sibling)

    def quarter_copy(i, d):
        h = (1 - xlo, 1 - xlo, xlo)[d]
        half = (rep, 1 - rep, 1 - rep)[d]
        return remote(tap.at[i, core, pl.ds((h * 2 + half) * 2, 2)], q_in.at[i, d],
                      q_s.at[i, d], q_r.at[i, d], x_peers[d])

    def eighth(i, z_at):
        rows = pl.ds(pl.multiple_of(lax.rem(z_at, 2) * 8, 8), 8)
        return tap.at[i, core, (xlo * 2 + rep) * 2 + lax.div(z_at, 2), rows]

    def eighth_copy(i, d):
        return remote(eighth(i, lax.rem(z + 1 + d, Z)), e_in.at[i, d],
                      e_s.at[i, d], e_r.at[i, d], z_peers[d])

    def swap_copy(i, which):
        part = fin.at[pl.ds(pl.multiple_of(which * 8, 8), 8), cols(i)]
        return remote(part, part, h_s.at[i], h_r.at[i], x_far)

    def stage_quarter(i):
        for d in range(3):
            quarter_copy(i, d).wait_recv()
        mine = pl.ds((xlo * 2 + rep) * 2, 2)
        tap[i, core, mine] = (tap[i, core, mine] + q_in[i, 0]) + (q_in[i, 1] + q_in[i, 2])
        for d in range(Z - 1):
            eighth_copy(i, d).start()

    def stage_eighth(i):
        for d in range(Z - 1):
            eighth_copy(i, d).wait_recv()
        total = (eighth(i, z)[...] + e_in[i, 0]) + (e_in[i, 1] + e_in[i, 2])
        fin[pl.ds(pl.multiple_of(rep * 8, 8), 8), cols(i)] = total
        swap_copy(i, rep).start()

    def z_copy(i, d):
        piece = pl.ds(lax.rem(z + 1 + d, Z) * 2, 2)
        at = i - x_first
        return remote(tap.at[i, core, piece], z_in.at[at, d], z_s.at[at, d], z_r.at[at, d], z_peers[d])

    def x_copy(i, d):
        h = (1 - xlo, 1 - xlo, xlo)[d]
        at = i - x_first
        return remote(tap.at[i, core, z * 2 + h], x_in.at[at, d], x_s.at[at, d], x_r.at[at, d], x_peers[d])

    def stage_swap(i):
        swap_copy(i, 1 - rep).wait_recv()

    def stage_pair(i):
        pair_copy(i).wait_recv()
        tap[i, core] += pair_in[i]

        @pl.when(i < x_first)
        def _():
            for d in range(3):
                quarter_copy(i, d).start()

        @pl.when(i >= x_first)
        def _():
            for d in range(Z - 1):
                z_copy(i, d).start()

    def stage_z(i):
        at = i - x_first
        for d in range(Z - 1):
            z_copy(i, d).wait_recv()
        mine = pl.ds(z * 2, 2)
        tap[i, core, mine] = (tap[i, core, mine] + z_in[at, 0]) + (z_in[at, 1] + z_in[at, 2])
        for d in range(3):
            x_copy(i, d).start()

    def stage_x(i):
        at = i - x_first
        for d in range(3):
            x_copy(i, d).wait_recv()
        fin[:, cols(i)] = (tap[i, core, z * 2 + xlo] + x_in[at, 2]) + (x_in[at, 0] + x_in[at, 1])

    for b in range(4):
        rows = lax.broadcasted_iota(jnp.int32, (REACH, TILE), 0) + b * REACH
        live_ref[pl.ds(b * REACH, REACH), :] = jnp.where(rows < live_count, 1.0, 0.0).astype(jnp.bfloat16)
    loads[0].wait()

    def mask_tail(i, carry):
        gbuf[pl.ds(384, 128), cols(i)] = gbuf[pl.ds(384, 128), cols(i)] * live_ref[pl.ds(384, 128), :]
        return carry

    lax.fori_loop(0, tiles, mask_tail, None)
    pl.semaphore_wait(barrier, len(peers))

    def send_halo(slot):
        i = tile_at(slot)

        @pl.when(ctx < ends - 1)
        def _():
            halo_right(i).start()

        @pl.when(ctx > 0)
        def _():
            halo_left(i).start()

    for c in range(chunks):
        for d in range(Z - 1):
            taps_z(c, d).start()

    @pl.when(ctx == 0)
    def _():
        from_left[...] = jnp.zeros_like(from_left)

    @pl.when(ctx == ends - 1)
    def _():
        from_right[...] = jnp.zeros_like(from_right)

    for copy in loads[2:5]:
        copy.wait()

    def analyse(b, block):
        return jnp.dot(ana_ref[b % 4], jnp.concatenate([block, block], 0),
                       preferred_element_type=jnp.float32)

    def put(ref, at, row, value):
        high, low = split(value)
        ref[at, pl.ds(row, STEP), :] = high
        ref[at, pl.ds(256 + row, STEP), :] = low

    def synthesise(table, spectrum, at):
        terms = jnp.concatenate([spectrum[at], spectrum[at, pl.ds(0, 256), :]], 0)
        return jnp.dot(table, terms, preferred_element_type=jnp.float32)

    def own_tile(i, carry):
        for b in range(4):
            rows = pl.ds(b * REACH, REACH)
            g_block, x_block = gbuf[rows, cols(i)], xbuf[rows, cols(i)]
            if b > 0:
                x_block = x_block * live_ref[rows, :]
            if b in (1, 2):
                g_block = g_block * live_ref[rows, :]
            af[i, b + 1] = analyse(b + 1, g_block)
            xf[i, b] = analyse(b, x_block)

        for part in range(2):
            slot = 2 * (i - HALO_FROM) + part

            @pl.when(jnp.logical_and(slot >= 0, slot < tiles))
            def _(slot=slot):
                send_halo(slot)

        return carry

    lax.fori_loop(0, tiles, own_tile, None)
    loads[1].wait()
    for c in range(chunks):
        taps_to_x(c)
    loads[5].wait()
    loads[6].wait()

    def windows(i, re, im):
        ar = [af[i, b, re, :] for b in range(6)]
        ai = [af[i, b, im, :] for b in range(6)]
        return [ar[b] + ar[b + 1] for b in range(5)], [ai[b] + ai[b + 1] for b in range(5)]

    def tap_tile(slot, carry):
        i = tile_at(slot)

        @pl.when(ctx > 0)
        def _():
            halo_right(i).wait_recv()

        @pl.when(ctx < ends - 1)
        def _():
            halo_left(i).wait_recv()

        af[i, 0] = analyse(0, from_left[i])
        af[i, 5] = analyse(5, from_right[i])

        def chunk(c, carry):
            row = pl.multiple_of(c * STEP, STEP)
            re, im = pl.ds(row, STEP), pl.ds(128 + row, STEP)
            gr, gi = windows(i, re, im)
            for h in range(2):
                tr = ti = None
                for b in range(4):
                    xr, xi = xf[i, b, re, :], xf[i, b, im, :]
                    pr = xr * gr[b + h] + xi * gi[b + h]
                    pi = xr * gi[b + h] - xi * gr[b + h]
                    tr, ti = (pr, pi) if tr is None else (tr + pr, ti + pi)
                put(tf, h, row, tr)
                put(tf, h, 128 + row, ti)
            return carry

        lax.fori_loop(0, 128 // STEP, chunk, None, unroll=True)
        for h in range(2):
            kind = jnp.where(i < x_first, 0, 1)
            terms = synthesise(tsyn_ref[kind, h], tf, h)
            for core_at in range(2):
                for u in range(4):
                    start = core_at * 64 + u * 16
                    unit = jnp.where(i < x_first, h * 4 + u, u * 2 + h)
                    tap[i, core_at, unit] = terms[start:start + 16]
        pair_copy(i).start()

        @pl.when(slot >= 1)
        def _():
            stage_pair(tile_at(slot - 1))

        @pl.when(slot >= tiles - 2)
        def _():
            taps_to_pair(slot - (tiles - 2))

        return carry

    lax.fori_loop(0, tiles, tap_tile, None)
    stage_pair(tiles - 1)
    for c in range(2, chunks):
        taps_to_pair(c)

    stages = {"quarter": stage_quarter, "eighth": stage_eighth, "swap": stage_swap,
              "z": stage_z, "x": stage_x}
    plan = reduction_plan(tiles, x_first, chunks)

    def weigh(i, at, spectrum):
        def chunk(c, carry):
            row = pl.multiple_of(c * STEP, STEP)
            re, im = pl.ds(row, STEP), pl.ds(128 + row, STEP)
            gr, gi = windows(i, re, im)
            w0r, w0i = wf[at, re, :], wf[at, im, :]
            w1r, w1i = wf[at + 1, re, :], wf[at + 1, im, :]
            for b in range(4):
                yr = (w0r * gr[b] + w0i * gi[b]) + (w1r * gr[b + 1] + w1i * gi[b + 1])
                yi = (w0r * gi[b] - w0i * gr[b]) + (w1r * gi[b + 1] - w1i * gr[b + 1])
                put(spectrum, b, row, yr)
                put(spectrum, b, 128 + row, yi)
            return carry

        lax.fori_loop(0, 128 // STEP, chunk, None, unroll=True)

    def emit(i, spectrum):
        for b in range(4):
            rows = pl.ds(b * REACH, REACH)
            value = synthesise(syn_ref[b], spectrum, b).astype(jnp.bfloat16)
            if b > 0:
                value = value * live_ref[rows, :]
            out_ref[0, rows, cols(i)] = value

    def grad_tiles(c, carry):
        taps_pair(c, 1 - core).wait_recv()
        first, second = 2 * c, 2 * c + 1
        for half, i in ((0, first), (1, second)):
            for h in range(2):
                block = wbuf[h, :, :, :, cols(i)].reshape(REACH, TILE)
                wf[half * 2 + h] = analyse(h, block)
        weigh(first, 0, ya)
        weigh(second, 2, yb)
        emit(first, ya)
        emit(second, yb)

        for at in range(chunks):
            @pl.when(c == at)
            def _(at=at):
                for stage, tile in plan[at]:
                    stages[stage](tile)

        return carry

    lax.fori_loop(0, chunks, grad_tiles, None)
    for stage, tile in plan[-1]:
        stages[stage](tile)
    tap_out[...] = fin[...]

    def finish(i, carry):
        pair_copy(i).wait_send()

        @pl.when(i < x_first)
        def _():
            for d in range(3):
                quarter_copy(i, d).wait_send()
                eighth_copy(i, d).wait_send()
            swap_copy(i, rep).wait_send()

        @pl.when(i >= x_first)
        def _():
            for d in range(3):
                z_copy(i, d).wait_send()
                x_copy(i, d).wait_send()

        @pl.when(ctx < ends - 1)
        def _():
            halo_right(i).wait_send()

        @pl.when(ctx > 0)
        def _():
            halo_left(i).wait_send()

        return carry

    lax.fori_loop(0, tiles, finish, None)
    for c in range(chunks):
        for d in range(Z - 1):
            taps_z(c, d).wait_send()
        for d in range(2):
            taps_x(c, d, xlo).wait_send()
        taps_pair(c, core).wait_send()


def fused(counts, x, g, taps):
    _, rows, channels = x.shape
    tiles = channels // TILE
    ana, syn, tsyn = transform_tables()
    dma = pltpu.SemaphoreType.DMA
    hbm = pl.BlockSpec(memory_space=pl.ANY)
    f32, bf16 = jnp.float32, jnp.bfloat16
    vmem = pl.BlockSpec(memory_space=pltpu.VMEM)
    first, rest = X_FIRST, tiles - X_FIRST
    return pl.pallas_call(
        functools.partial(kernel, tiles),
        out_shape=(pltpu.VMEM(x.shape, bf16), pltpu.VMEM(taps.shape, f32)),
        in_specs=[pl.BlockSpec(memory_space=pltpu.SMEM)] + [hbm] * 6,
        out_specs=(vmem, vmem),
        scratch_shapes=[
            pltpu.VMEM(ana.shape, bf16),
            pltpu.VMEM(syn.shape, bf16),
            pltpu.VMEM(tsyn.shape, bf16),
            pltpu.VMEM((rows, TILE), bf16),
            pltpu.VMEM((rows, channels), bf16),
            pltpu.VMEM((rows, channels), bf16),
            pltpu.VMEM((tiles, REACH, TILE), bf16),
            pltpu.VMEM((tiles, REACH, TILE), bf16),
            pltpu.VMEM((2, Z, 2, 16, channels), bf16),
            pltpu.VMEM((tiles, 6, 256, TILE), f32),
            pltpu.VMEM((tiles, 4, 256, TILE), f32),
            pltpu.VMEM((4, 256, TILE), f32),
            pltpu.VMEM((4, 512, TILE), bf16),
            pltpu.VMEM((4, 512, TILE), bf16),
            pltpu.VMEM((2, 512, TILE), bf16),
            pltpu.VMEM((tiles, 2, 8, 16, TILE), f32),
            pltpu.VMEM((tiles, 8, 16, TILE), f32),
            pltpu.VMEM((first, 3, 2, 16, TILE), f32),
            pltpu.VMEM((first, 3, 8, TILE), f32),
            pltpu.VMEM((rest, 3, 2, 16, TILE), f32),
            pltpu.VMEM((rest, 3, 16, TILE), f32),
            pltpu.VMEM((16, channels), f32),
            dma((8,)),
            dma((2, tiles)), dma((2, tiles)),
            dma((tiles // 2, 3)), dma((tiles // 2, 3)),
            dma((tiles // 2, 2)), dma((tiles // 2, 2)),
            dma((tiles // 2,)), dma((tiles // 2,)),
            dma((tiles,)), dma((tiles,)),
            dma((first, 3)), dma((first, 3)),
            dma((first, 3)), dma((first, 3)),
            dma((first,)), dma((first,)),
            dma((rest, 3)), dma((rest, 3)),
            dma((rest, 3)), dma((rest, 3)),
        ],
        compiler_params=pltpu.CompilerParams(
            collective_id=0, has_side_effects=True, vmem_limit_bytes=56 << 20),
    )(counts, jnp.asarray(ana), jnp.asarray(syn), jnp.asarray(tsyn), x, g, taps)


def local(saved_input, out_grad, filter_taps, valid_counts):
    return fused(valid_counts, saved_input, out_grad, filter_taps)


def solution(mesh):
    return jax.shard_map(
        local,
        mesh=mesh,
        in_specs=(P("rep", "ctx", "ch"), P("rep", "ctx", "ch"), P("ctx", "ch"), P("rep", "ctx")),
        out_specs=(P("rep", "ctx", "ch"), P("ctx", "ch")),
        check_vma=False,
    )
```

```python
import functools
import math

import jax
import jax.numpy as jnp
import numpy as np
from jax import lax
from jax.experimental import pallas as pl
from jax.experimental.pallas import tpu as pltpu
from jax.sharding import PartitionSpec as P

REACH = 128
TILE = 256
STEP = 16
X_FIRST = 3
HALO_FROM = 0
Z = 4


def transform_tables():
    freq = 2 * np.arange(128)[:, None] + 1
    analysis, synthesis = [], []
    for b in range(4):
        angle = np.pi * (freq * (np.arange(128)[None, :] + 128 * b) % 512) / 256.0
        forward = np.concatenate([np.cos(angle), -np.sin(angle)], 0)
        high = forward.astype(jnp.bfloat16)
        low = (forward - high.astype(np.float64)).astype(jnp.bfloat16)
        analysis.append(np.concatenate([high, low], 1))
        back = [part.astype(np.float64).T / 128 for part in (high, high, low)]
        synthesis.append(np.concatenate(back, 1))
    x_rows = [32 * z + 16 * core + 8 * half + r
              for core in range(2) for half in range(2) for z in range(Z) for r in range(8)]
    z_rows = [32 * z + 16 * core + r for core in range(2) for z in range(Z) for r in range(16)]
    tap_scale = 1.0 / 128
    taps = np.stack([np.stack([synthesis[h][rows] * tap_scale for h in range(2)])
                     for rows in (x_rows, z_rows)])
    return (np.stack(analysis), np.stack(synthesis).astype(jnp.bfloat16), taps.astype(jnp.bfloat16))


def reduction_plan(tiles, x_first, chunks):
    early, late = list(range(x_first)), list(range(x_first, tiles))
    cut = (x_first + 1) // 2
    plan = [[("z", i) for i in late[4:5]] + [("eighth", i) for i in early[:cut]],
            [("eighth", i) for i in early[cut:]],
            [],
            [],
            [("x", i) for i in late] + [("swap", i) for i in early],
            [("quarter", i) for i in early[:cut]] + [("z", i) for i in late[:2]]
            + [("quarter", i) for i in early[cut:]],
            [("z", i) for i in late[2:4]]]
    assert len(plan) == chunks + 3
    return plan


def split(value):
    high = value.astype(jnp.bfloat16)
    low = (value - high.astype(jnp.float32)).astype(jnp.bfloat16)
    return high, low


def kernel(tiles, count_ref, ana_hbm, syn_hbm, tsyn_hbm, x_hbm, g_hbm, w_hbm,
           out_ref, tap_out,
           ana_ref, syn_ref, tsyn_ref, live_ref, gbuf, xbuf, from_left, from_right, wbuf,
           af, xf, wf, ya, yb, tf, tap, pair_in, q_in, e_in, z_in, x_in, fin,
           load_sem, halo_s, halo_r, wz_s, wz_r, wx_s, wx_r, wp_s, wp_r,
           p_s, p_r, q_s, q_r, e_s, e_r, h_s, h_r, z_s, z_r, x_s, x_r):
    live_count = count_ref[0, 0]
    ctx = lax.axis_index("ctx")
    rep = lax.axis_index("rep")
    ends = 16
    core = lax.rem(ctx, 2)
    z = lax.rem(lax.div(ctx, 2), Z)
    xlo = lax.div(ctx, 8)
    chunks = tiles // 2
    x_first = X_FIRST

    def device(x_lo, z_at, core_at, rep_at):
        return {"ctx": x_lo * 8 + z_at * 2 + core_at, "rep": rep_at}

    def remote(src, dst, send, recv, target):
        return pltpu.make_async_remote_copy(
            src_ref=src, dst_ref=dst, send_sem=send, recv_sem=recv,
            device_id=target, device_id_type=pl.DeviceIdType.MESH)

    left = {"ctx": lax.rem(ctx + ends - 1, ends), "rep": rep}
    right = {"ctx": lax.rem(ctx + 1, ends), "rep": rep}
    sibling = device(xlo, z, 1 - core, rep)
    x_near = device(1 - xlo, z, core, rep)
    x_wrap = device(1 - xlo, z, core, 1 - rep)
    x_far = device(xlo, z, core, 1 - rep)
    x_peers = (x_near, x_wrap, x_far)
    z_peers = [device(xlo, lax.rem(z + d, Z), core, rep) for d in range(1, Z)]

    barrier = pltpu.get_barrier_semaphore()
    peers = [left, right, x_near, x_wrap, x_far] + z_peers
    for peer in peers:
        pl.semaphore_signal(barrier, inc=1, device_id=peer, device_id_type=pl.DeviceIdType.MESH)

    loads = [
        pltpu.make_async_copy(g_hbm.at[0, pl.ds(384, 128), :], gbuf.at[pl.ds(384, 128), :], load_sem.at[0]),
        pltpu.make_async_copy(w_hbm, wbuf.at[xlo, z, core], load_sem.at[1]),
        pltpu.make_async_copy(g_hbm.at[0, pl.ds(0, 384), :], gbuf.at[pl.ds(0, 384), :], load_sem.at[2]),
        pltpu.make_async_copy(x_hbm.at[0], xbuf, load_sem.at[3]),
        pltpu.make_async_copy(ana_hbm, ana_ref, load_sem.at[4]),
        pltpu.make_async_copy(tsyn_hbm, tsyn_ref, load_sem.at[5]),
        pltpu.make_async_copy(syn_hbm, syn_ref, load_sem.at[6]),
    ]
    for copy in loads:
        copy.start()

    def cols(i):
        return pl.ds(pl.multiple_of(i * TILE, TILE), TILE)

    def tile_at(slot):
        mixed = lax.rem(slot, 2) * x_first + lax.div(slot, 2)
        return jnp.where(slot < 2 * x_first, mixed, slot)

    def halo_right(i):
        return remote(gbuf.at[pl.ds(384, 128), cols(i)], from_left.at[i],
                      halo_s.at[0, i], halo_r.at[0, i], right)

    def halo_left(i):
        return remote(g_hbm.at[0, pl.ds(0, 128), cols(i)], from_right.at[i],
                      halo_s.at[1, i], halo_r.at[1, i], left)

    def pair_cols(c):
        return pl.ds(pl.multiple_of(c * 2 * TILE, 2 * TILE), 2 * TILE)

    def taps_z(c, d):
        return remote(w_hbm.at[:, pair_cols(c)], wbuf.at[xlo, z, core, :, pair_cols(c)],
                      wz_s.at[c, d], wz_r.at[c, d], z_peers[d])

    def taps_z_arrival(c, d):
        source = lax.rem(z + Z - 1 - d, Z)
        return remote(w_hbm.at[:, pair_cols(c)], wbuf.at[xlo, source, core, :, pair_cols(c)],
                      wz_s.at[c, d], wz_r.at[c, d], z_peers[d])

    def taps_x(c, d, which):
        part = wbuf.at[which, :, core, :, cols(2 * c + d)]
        return remote(part, part, wx_s.at[c, d], wx_r.at[c, d], x_peers[d])

    def taps_pair(c, which):
        part = wbuf.at[:, :, which, :, pair_cols(c)]
        return remote(part, part, wp_s.at[c], wp_r.at[c], sibling)

    def taps_to_x(c):
        for d in range(Z - 1):
            taps_z_arrival(c, d).wait_recv()
        for d in range(2):
            taps_x(c, d, xlo).start()

    def taps_to_pair(c):
        for d in range(2):
            taps_x(c, d, 1 - xlo).wait_recv()
        taps_pair(c, core).start()

    def pair_copy(i):
        return remote(tap.at[i, 1 - core], pair_in.at[i], p_s.at[i], p_r.at[i], sibling)

    def quarter_copy(i, d):
        h = (1 - xlo, 1 - xlo, xlo)[d]
        half = (rep, 1 - rep, 1 - rep)[d]
        return remote(tap.at[i, core, pl.ds((h * 2 + half) * 2, 2)], q_in.at[i, d],
                      q_s.at[i, d], q_r.at[i, d], x_peers[d])

    def eighth(i, z_at):
        rows = pl.ds(pl.multiple_of(lax.rem(z_at, 2) * 8, 8), 8)
        return tap.at[i, core, (xlo * 2 + rep) * 2 + lax.div(z_at, 2), rows]

    def eighth_copy(i, d):
        return remote(eighth(i, lax.rem(z + 1 + d, Z)), e_in.at[i, d],
                      e_s.at[i, d], e_r.at[i, d], z_peers[d])

    def swap_copy(i, which):
        part = fin.at[pl.ds(pl.multiple_of(which * 8, 8), 8), cols(i)]
        return remote(part, part, h_s.at[i], h_r.at[i], x_far)

    def stage_quarter(i):
        for d in range(3):
            quarter_copy(i, d).wait_recv()
        mine = pl.ds((xlo * 2 + rep) * 2, 2)
        tap[i, core, mine] = (tap[i, core, mine] + q_in[i, 0]) + (q_in[i, 1] + q_in[i, 2])
        for d in range(Z - 1):
            eighth_copy(i, d).start()

    def stage_eighth(i):
        for d in range(Z - 1):
            eighth_copy(i, d).wait_recv()
        total = (eighth(i, z)[...] + e_in[i, 0]) + (e_in[i, 1] + e_in[i, 2])
        fin[pl.ds(pl.multiple_of(rep * 8, 8), 8), cols(i)] = total
        swap_copy(i, rep).start()

    def z_copy(i, d):
        piece = pl.ds(lax.rem(z + 1 + d, Z) * 2, 2)
        at = i - x_first
        return remote(tap.at[i, core, piece], z_in.at[at, d], z_s.at[at, d], z_r.at[at, d], z_peers[d])

    def x_copy(i, d):
        h = (1 - xlo, 1 - xlo, xlo)[d]
        at = i - x_first
        return remote(tap.at[i, core, z * 2 + h], x_in.at[at, d], x_s.at[at, d], x_r.at[at, d], x_peers[d])

    def stage_swap(i):
        swap_copy(i, 1 - rep).wait_recv()

    def stage_pair(i):
        pair_copy(i).wait_recv()
        tap[i, core] += pair_in[i]

        @pl.when(i < x_first)
        def _():
            for d in range(3):
                quarter_copy(i, d).start()

        @pl.when(i >= x_first)
        def _():
            for d in range(Z - 1):
                z_copy(i, d).start()

    def stage_z(i):
        at = i - x_first
        for d in range(Z - 1):
            z_copy(i, d).wait_recv()
        mine = pl.ds(z * 2, 2)
        tap[i, core, mine] = (tap[i, core, mine] + z_in[at, 0]) + (z_in[at, 1] + z_in[at, 2])
        for d in range(3):
            x_copy(i, d).start()

    def stage_x(i):
        at = i - x_first
        for d in range(3):
            x_copy(i, d).wait_recv()
        fin[:, cols(i)] = (tap[i, core, z * 2 + xlo] + x_in[at, 2]) + (x_in[at, 0] + x_in[at, 1])

    for b in range(4):
        rows = lax.broadcasted_iota(jnp.int32, (REACH, TILE), 0) + b * REACH
        live_ref[pl.ds(b * REACH, REACH), :] = jnp.where(rows < live_count, 1.0, 0.0).astype(jnp.bfloat16)
    loads[0].wait()

    def mask_tail(i, carry):
        gbuf[pl.ds(384, 128), cols(i)] = gbuf[pl.ds(384, 128), cols(i)] * live_ref[pl.ds(384, 128), :]
        return carry

    lax.fori_loop(0, tiles, mask_tail, None)
    pl.semaphore_wait(barrier, len(peers))

    def send_halo(slot):
        i = tile_at(slot)

        @pl.when(ctx < ends - 1)
        def _():
            halo_right(i).start()

        @pl.when(ctx > 0)
        def _():
            halo_left(i).start()


    @pl.when(ctx == 0)
    def _():
        from_left[...] = jnp.zeros_like(from_left)

    @pl.when(ctx == ends - 1)
    def _():
        from_right[...] = jnp.zeros_like(from_right)

    for copy in loads[2:5]:
        copy.wait()

    def analyse(b, block):
        return jnp.dot(ana_ref[b % 4], jnp.concatenate([block, block], 0),
                       preferred_element_type=jnp.float32)

    def put(ref, at, row, value):
        high, low = split(value)
        ref[at, pl.ds(row, STEP), :] = high
        ref[at, pl.ds(256 + row, STEP), :] = low

    def synthesise(table, spectrum, at):
        terms = jnp.concatenate([spectrum[at], spectrum[at, pl.ds(0, 256), :]], 0)
        return jnp.dot(table, terms, preferred_element_type=jnp.float32)

    def own_tile(i, carry):
        for b in range(4):
            rows = pl.ds(b * REACH, REACH)
            g_block, x_block = gbuf[rows, cols(i)], xbuf[rows, cols(i)]
            if b > 0:
                x_block = x_block * live_ref[rows, :]
            if b in (1, 2):
                g_block = g_block * live_ref[rows, :]
            af[i, b + 1] = analyse(b + 1, g_block)
            xf[i, b] = analyse(b, x_block)

        for part in range(2):
            slot = 2 * (i - HALO_FROM) + part

            @pl.when(jnp.logical_and(slot >= 0, slot < tiles))
            def _(slot=slot):
                send_halo(slot)

        return carry

    lax.fori_loop(0, tiles, own_tile, None)
    for c in range(chunks):
        for d in range(Z - 1):
            taps_z(c, d).start()
    loads[1].wait()
    loads[5].wait()
    loads[6].wait()

    def windows(i, re, im):
        ar = [af[i, b, re, :] for b in range(6)]
        ai = [af[i, b, im, :] for b in range(6)]
        return [ar[b] + ar[b + 1] for b in range(5)], [ai[b] + ai[b + 1] for b in range(5)]

    def tap_tile(slot, carry):
        i = tile_at(slot)

        @pl.when(ctx > 0)
        def _():
            halo_right(i).wait_recv()

        @pl.when(ctx < ends - 1)
        def _():
            halo_left(i).wait_recv()

        af[i, 0] = analyse(0, from_left[i])
        af[i, 5] = analyse(5, from_right[i])

        def chunk(c, carry):
            row = pl.multiple_of(c * STEP, STEP)
            re, im = pl.ds(row, STEP), pl.ds(128 + row, STEP)
            gr, gi = windows(i, re, im)
            for h in range(2):
                tr = ti = None
                for b in range(4):
                    xr, xi = xf[i, b, re, :], xf[i, b, im, :]
                    pr = xr * gr[b + h] + xi * gi[b + h]
                    pi = xr * gi[b + h] - xi * gr[b + h]
                    tr, ti = (pr, pi) if tr is None else (tr + pr, ti + pi)
                put(tf, h, row, tr)
                put(tf, h, 128 + row, ti)
            return carry

        lax.fori_loop(0, 128 // STEP, chunk, None, unroll=True)
        for h in range(2):
            kind = jnp.where(i < x_first, 0, 1)
            terms = synthesise(tsyn_ref[kind, h], tf, h)
            for core_at in range(2):
                for u in range(4):
                    start = core_at * 64 + u * 16
                    unit = jnp.where(i < x_first, h * 4 + u, u * 2 + h)
                    tap[i, core_at, unit] = terms[start:start + 16]
        pair_copy(i).start()

        @pl.when(slot >= 2)
        def _():
            stage_pair(tile_at(slot - 2))


        return carry

    lax.fori_loop(0, tiles, tap_tile, None)
    stages = {"quarter": stage_quarter, "eighth": stage_eighth, "swap": stage_swap,
              "z": stage_z, "x": stage_x}
    plan = reduction_plan(tiles, x_first, chunks)

    stage_pair(tiles - 2)
    for c in range(chunks):
        taps_to_x(c)
    stage_pair(tiles - 1)
    for stage, tile in plan[chunks + 1]:
        stages[stage](tile)
    for c in range(chunks):
        taps_to_pair(c)
    for stage, tile in plan[chunks + 2]:
        stages[stage](tile)


    def weigh(i, at, spectrum):
        def chunk(c, carry):
            row = pl.multiple_of(c * STEP, STEP)
            re, im = pl.ds(row, STEP), pl.ds(128 + row, STEP)
            gr, gi = windows(i, re, im)
            w0r, w0i = wf[at, re, :], wf[at, im, :]
            w1r, w1i = wf[at + 1, re, :], wf[at + 1, im, :]
            for b in range(4):
                yr = (w0r * gr[b] + w0i * gi[b]) + (w1r * gr[b + 1] + w1i * gi[b + 1])
                yi = (w0r * gi[b] - w0i * gr[b]) + (w1r * gi[b + 1] - w1i * gr[b + 1])
                put(spectrum, b, row, yr)
                put(spectrum, b, 128 + row, yi)
            return carry

        lax.fori_loop(0, 128 // STEP, chunk, None, unroll=True)

    def emit(i, spectrum):
        for b in range(4):
            rows = pl.ds(b * REACH, REACH)
            value = synthesise(syn_ref[b], spectrum, b).astype(jnp.bfloat16)
            if b > 0:
                value = value * live_ref[rows, :]
            out_ref[0, rows, cols(i)] = value

    def grad_tiles(c, carry):
        taps_pair(c, 1 - core).wait_recv()
        first, second = 2 * c, 2 * c + 1
        for half, i in ((0, first), (1, second)):
            for h in range(2):
                block = wbuf[h, :, :, :, cols(i)].reshape(REACH, TILE)
                wf[half * 2 + h] = analyse(h, block)
        weigh(first, 0, ya)
        weigh(second, 2, yb)
        emit(first, ya)
        emit(second, yb)

        for at in range(chunks):
            @pl.when(c == at)
            def _(at=at):
                for stage, tile in plan[at]:
                    stages[stage](tile)

        return carry

    lax.fori_loop(0, chunks, grad_tiles, None)
    for stage, tile in plan[chunks]:
        stages[stage](tile)
    tap_out[...] = fin[...]

    def finish(i, carry):
        pair_copy(i).wait_send()

        @pl.when(i < x_first)
        def _():
            for d in range(3):
                quarter_copy(i, d).wait_send()
                eighth_copy(i, d).wait_send()
            swap_copy(i, rep).wait_send()

        @pl.when(i >= x_first)
        def _():
            for d in range(3):
                z_copy(i, d).wait_send()
                x_copy(i, d).wait_send()

        @pl.when(ctx < ends - 1)
        def _():
            halo_right(i).wait_send()

        @pl.when(ctx > 0)
        def _():
            halo_left(i).wait_send()

        return carry

    lax.fori_loop(0, tiles, finish, None)
    for c in range(chunks):
        for d in range(Z - 1):
            taps_z(c, d).wait_send()
        for d in range(2):
            taps_x(c, d, xlo).wait_send()
        taps_pair(c, core).wait_send()


def fused(counts, x, g, taps):
    _, rows, channels = x.shape
    tiles = channels // TILE
    ana, syn, tsyn = transform_tables()
    dma = pltpu.SemaphoreType.DMA
    hbm = pl.BlockSpec(memory_space=pl.ANY)
    f32, bf16 = jnp.float32, jnp.bfloat16
    vmem = pl.BlockSpec(memory_space=pltpu.VMEM)
    first, rest = X_FIRST, tiles - X_FIRST
    return pl.pallas_call(
        functools.partial(kernel, tiles),
        out_shape=(pltpu.VMEM(x.shape, bf16), pltpu.VMEM(taps.shape, f32)),
        in_specs=[pl.BlockSpec(memory_space=pltpu.SMEM)] + [hbm] * 6,
        out_specs=(vmem, vmem),
        scratch_shapes=[
            pltpu.VMEM(ana.shape, bf16),
            pltpu.VMEM(syn.shape, bf16),
            pltpu.VMEM(tsyn.shape, bf16),
            pltpu.VMEM((rows, TILE), bf16),
            pltpu.VMEM((rows, channels), bf16),
            pltpu.VMEM((rows, channels), bf16),
            pltpu.VMEM((tiles, REACH, TILE), bf16),
            pltpu.VMEM((tiles, REACH, TILE), bf16),
            pltpu.VMEM((2, Z, 2, 16, channels), bf16),
            pltpu.VMEM((tiles, 6, 256, TILE), f32),
            pltpu.VMEM((tiles, 4, 256, TILE), f32),
            pltpu.VMEM((4, 256, TILE), f32),
            pltpu.VMEM((4, 512, TILE), bf16),
            pltpu.VMEM((4, 512, TILE), bf16),
            pltpu.VMEM((2, 512, TILE), bf16),
            pltpu.VMEM((tiles, 2, 8, 16, TILE), f32),
            pltpu.VMEM((tiles, 8, 16, TILE), f32),
            pltpu.VMEM((first, 3, 2, 16, TILE), f32),
            pltpu.VMEM((first, 3, 8, TILE), f32),
            pltpu.VMEM((rest, 3, 2, 16, TILE), f32),
            pltpu.VMEM((rest, 3, 16, TILE), f32),
            pltpu.VMEM((16, channels), f32),
            dma((8,)),
            dma((2, tiles)), dma((2, tiles)),
            dma((tiles // 2, 3)), dma((tiles // 2, 3)),
            dma((tiles // 2, 2)), dma((tiles // 2, 2)),
            dma((tiles // 2,)), dma((tiles // 2,)),
            dma((tiles,)), dma((tiles,)),
            dma((first, 3)), dma((first, 3)),
            dma((first, 3)), dma((first, 3)),
            dma((first,)), dma((first,)),
            dma((rest, 3)), dma((rest, 3)),
            dma((rest, 3)), dma((rest, 3)),
        ],
        compiler_params=pltpu.CompilerParams(
            collective_id=0, has_side_effects=True, vmem_limit_bytes=56 << 20),
    )(counts, jnp.asarray(ana), jnp.asarray(syn), jnp.asarray(tsyn), x, g, taps)


def local(saved_input, out_grad, filter_taps, valid_counts):
    return fused(valid_counts, saved_input, out_grad, filter_taps)


def solution(mesh):
    return jax.shard_map(
        local,
        mesh=mesh,
        in_specs=(P("rep", "ctx", "ch"), P("rep", "ctx", "ch"), P("ctx", "ch"), P("rep", "ctx")),
        out_specs=(P("rep", "ctx", "ch"), P("ctx", "ch")),
        check_vma=False,
    )
```

```python
import functools
import math

import jax
import jax.numpy as jnp
import numpy as np
from jax import lax
from jax.experimental import pallas as pl
from jax.experimental.pallas import tpu as pltpu
from jax.sharding import PartitionSpec as P

REACH = 128
TILE = 256
STEP = 16
X_FIRST = 3
HALO_FROM = 0
Z = 4


def transform_tables():
    freq = 2 * np.arange(128)[:, None] + 1
    analysis, synthesis = [], []
    for b in range(4):
        angle = np.pi * (freq * (np.arange(128)[None, :] + 128 * b) % 512) / 256.0
        forward = np.concatenate([np.cos(angle), -np.sin(angle)], 0)
        high = forward.astype(jnp.bfloat16)
        low = (forward - high.astype(np.float64)).astype(jnp.bfloat16)
        analysis.append(np.concatenate([high, low], 1))
        back = [part.astype(np.float64).T / 128 for part in (high, high, low)]
        synthesis.append(np.concatenate(back, 1))
    x_rows = [32 * z + 16 * core + 8 * half + r
              for core in range(2) for half in range(2) for z in range(Z) for r in range(8)]
    z_rows = [32 * z + 16 * core + r for core in range(2) for z in range(Z) for r in range(16)]
    tap_scale = 1.0 / 128
    taps = np.stack([np.stack([synthesis[h][rows] * tap_scale for h in range(2)])
                     for rows in (x_rows, z_rows)])
    return (np.stack(analysis), np.stack(synthesis).astype(jnp.bfloat16), taps.astype(jnp.bfloat16))


def reduction_plan(tiles, x_first, chunks):
    early, late = list(range(x_first)), list(range(x_first, tiles))
    cut = (x_first + 1) // 2
    plan = [[("z", i) for i in late[4:5]] + [("eighth", i) for i in early[:cut]],
            [("eighth", i) for i in early[cut:]],
            [],
            [],
            [("x", i) for i in late] + [("swap", i) for i in early],
            [("quarter", i) for i in early[:cut]] + [("z", i) for i in late[:2]]
            + [("quarter", i) for i in early[cut:]],
            [("z", i) for i in late[2:4]]]
    assert len(plan) == chunks + 3
    return plan


def split(value):
    high = value.astype(jnp.bfloat16)
    low = (value - high.astype(jnp.float32)).astype(jnp.bfloat16)
    return high, low


def kernel(tiles, count_ref, ana_hbm, syn_hbm, tsyn_hbm, x_hbm, g_hbm, w_hbm,
           out_ref, tap_out,
           ana_ref, syn_ref, tsyn_ref, live_ref, gbuf, xbuf, from_left, from_right, wbuf,
           af, xf, wf, ya, yb, tf, tap, pair_in, q_in, e_in, z_in, x_in, fin,
           load_sem, halo_s, halo_r, wz_s, wz_r, wx_s, wx_r, wp_s, wp_r,
           p_s, p_r, q_s, q_r, e_s, e_r, h_s, h_r, z_s, z_r, x_s, x_r):
    live_count = count_ref[0, 0]
    ctx = lax.axis_index("ctx")
    rep = lax.axis_index("rep")
    ends = 16
    core = lax.rem(ctx, 2)
    z = lax.rem(lax.div(ctx, 2), Z)
    xlo = lax.div(ctx, 8)
    chunks = tiles // 2
    x_first = X_FIRST

    def device(x_lo, z_at, core_at, rep_at):
        return {"ctx": x_lo * 8 + z_at * 2 + core_at, "rep": rep_at}

    def remote(src, dst, send, recv, target):
        return pltpu.make_async_remote_copy(
            src_ref=src, dst_ref=dst, send_sem=send, recv_sem=recv,
            device_id=target, device_id_type=pl.DeviceIdType.MESH)

    left = {"ctx": lax.rem(ctx + ends - 1, ends), "rep": rep}
    right = {"ctx": lax.rem(ctx + 1, ends), "rep": rep}
    sibling = device(xlo, z, 1 - core, rep)
    x_near = device(1 - xlo, z, core, rep)
    x_wrap = device(1 - xlo, z, core, 1 - rep)
    x_far = device(xlo, z, core, 1 - rep)
    x_peers = (x_near, x_wrap, x_far)
    z_peers = [device(xlo, lax.rem(z + d, Z), core, rep) for d in range(1, Z)]

    barrier = pltpu.get_barrier_semaphore()
    peers = [left, right, x_near, x_wrap, x_far] + z_peers
    for peer in peers:
        pl.semaphore_signal(barrier, inc=1, device_id=peer, device_id_type=pl.DeviceIdType.MESH)

    loads = [
        pltpu.make_async_copy(g_hbm.at[0, pl.ds(384, 128), :], gbuf.at[pl.ds(384, 128), :], load_sem.at[0]),
        pltpu.make_async_copy(w_hbm, wbuf.at[xlo, z, core], load_sem.at[1]),
        pltpu.make_async_copy(g_hbm.at[0, pl.ds(0, 384), :], gbuf.at[pl.ds(0, 384), :], load_sem.at[2]),
        pltpu.make_async_copy(x_hbm.at[0], xbuf, load_sem.at[3]),
        pltpu.make_async_copy(ana_hbm, ana_ref, load_sem.at[4]),
        pltpu.make_async_copy(tsyn_hbm, tsyn_ref, load_sem.at[5]),
        pltpu.make_async_copy(syn_hbm, syn_ref, load_sem.at[6]),
    ]
    for copy in loads:
        copy.start()

    def cols(i):
        return pl.ds(pl.multiple_of(i * TILE, TILE), TILE)

    def tile_at(slot):
        mixed = lax.rem(slot, 2) * x_first + lax.div(slot, 2)
        return jnp.where(slot < 2 * x_first, mixed, slot)

    def halo_right(i):
        return remote(gbuf.at[pl.ds(384, 128), cols(i)], from_left.at[i],
                      halo_s.at[0, i], halo_r.at[0, i], right)

    def halo_left(i):
        return remote(g_hbm.at[0, pl.ds(0, 128), cols(i)], from_right.at[i],
                      halo_s.at[1, i], halo_r.at[1, i], left)

    def pair_cols(c):
        return pl.ds(pl.multiple_of(c * 2 * TILE, 2 * TILE), 2 * TILE)

    def taps_z(c, d):
        return remote(w_hbm.at[:, pair_cols(c)], wbuf.at[xlo, z, core, :, pair_cols(c)],
                      wz_s.at[c, d], wz_r.at[c, d], z_peers[d])

    def taps_z_arrival(c, d):
        source = lax.rem(z + Z - 1 - d, Z)
        return remote(w_hbm.at[:, pair_cols(c)], wbuf.at[xlo, source, core, :, pair_cols(c)],
                      wz_s.at[c, d], wz_r.at[c, d], z_peers[d])

    def taps_x(c, d, which):
        part = wbuf.at[which, :, core, :, cols(2 * c + d)]
        return remote(part, part, wx_s.at[c, d], wx_r.at[c, d], x_peers[d])

    def taps_pair(c, which):
        part = wbuf.at[:, :, which, :, pair_cols(c)]
        return remote(part, part, wp_s.at[c], wp_r.at[c], sibling)

    def taps_to_x(c):
        for d in range(Z - 1):
            taps_z_arrival(c, d).wait_recv()
        for d in range(2):
            taps_x(c, d, xlo).start()

    def taps_to_pair(c):
        for d in range(2):
            taps_x(c, d, 1 - xlo).wait_recv()
        taps_pair(c, core).start()

    def pair_copy(i):
        return remote(tap.at[i, 1 - core], pair_in.at[i], p_s.at[i], p_r.at[i], sibling)

    def quarter_copy(i, d):
        h = (1 - xlo, 1 - xlo, xlo)[d]
        half = (rep, 1 - rep, 1 - rep)[d]
        return remote(tap.at[i, core, pl.ds((h * 2 + half) * 2, 2)], q_in.at[i, d],
                      q_s.at[i, d], q_r.at[i, d], x_peers[d])

    def eighth(i, z_at):
        rows = pl.ds(pl.multiple_of(lax.rem(z_at, 2) * 8, 8), 8)
        return tap.at[i, core, (xlo * 2 + rep) * 2 + lax.div(z_at, 2), rows]

    def eighth_copy(i, d):
        return remote(eighth(i, lax.rem(z + 1 + d, Z)), e_in.at[i, d],
                      e_s.at[i, d], e_r.at[i, d], z_peers[d])

    def swap_copy(i, which):
        part = fin.at[pl.ds(pl.multiple_of(which * 8, 8), 8), cols(i)]
        return remote(part, part, h_s.at[i], h_r.at[i], x_far)

    def stage_quarter(i):
        for d in range(3):
            quarter_copy(i, d).wait_recv()
        mine = pl.ds((xlo * 2 + rep) * 2, 2)
        tap[i, core, mine] = (tap[i, core, mine] + q_in[i, 0]) + (q_in[i, 1] + q_in[i, 2])
        for d in range(Z - 1):
            eighth_copy(i, d).start()

    def stage_eighth(i):
        for d in range(Z - 1):
            eighth_copy(i, d).wait_recv()
        total = (eighth(i, z)[...] + e_in[i, 0]) + (e_in[i, 1] + e_in[i, 2])
        fin[pl.ds(pl.multiple_of(rep * 8, 8), 8), cols(i)] = total
        swap_copy(i, rep).start()

    def z_copy(i, d):
        piece = pl.ds(lax.rem(z + 1 + d, Z) * 2, 2)
        at = i - x_first
        return remote(tap.at[i, core, piece], z_in.at[at, d], z_s.at[at, d], z_r.at[at, d], z_peers[d])

    def x_copy(i, d):
        h = (1 - xlo, 1 - xlo, xlo)[d]
        at = i - x_first
        return remote(tap.at[i, core, z * 2 + h], x_in.at[at, d], x_s.at[at, d], x_r.at[at, d], x_peers[d])

    def stage_swap(i):
        swap_copy(i, 1 - rep).wait_recv()

    def stage_pair(i):
        pair_copy(i).wait_recv()
        tap[i, core] += pair_in[i]

        @pl.when(i < x_first)
        def _():
            for d in range(3):
                quarter_copy(i, d).start()

        @pl.when(i >= x_first)
        def _():
            for d in range(Z - 1):
                z_copy(i, d).start()

    def stage_z(i):
        at = i - x_first
        for d in range(Z - 1):
            z_copy(i, d).wait_recv()
        mine = pl.ds(z * 2, 2)
        tap[i, core, mine] = (tap[i, core, mine] + z_in[at, 0]) + (z_in[at, 1] + z_in[at, 2])
        for d in range(3):
            x_copy(i, d).start()

    def stage_x(i):
        at = i - x_first
        for d in range(3):
            x_copy(i, d).wait_recv()
        fin[:, cols(i)] = (tap[i, core, z * 2 + xlo] + x_in[at, 2]) + (x_in[at, 0] + x_in[at, 1])

    for b in range(4):
        rows = lax.broadcasted_iota(jnp.int32, (REACH, TILE), 0) + b * REACH
        live_ref[pl.ds(b * REACH, REACH), :] = jnp.where(rows < live_count, 1.0, 0.0).astype(jnp.bfloat16)
    loads[0].wait()

    def mask_tail(i, carry):
        gbuf[pl.ds(384, 128), cols(i)] = gbuf[pl.ds(384, 128), cols(i)] * live_ref[pl.ds(384, 128), :]
        return carry

    lax.fori_loop(0, tiles, mask_tail, None)
    pl.semaphore_wait(barrier, len(peers))

    def send_halo(slot):
        i = tile_at(slot)

        @pl.when(ctx < ends - 1)
        def _():
            halo_right(i).start()

        @pl.when(ctx > 0)
        def _():
            halo_left(i).start()


    @pl.when(ctx == 0)
    def _():
        from_left[...] = jnp.zeros_like(from_left)

    @pl.when(ctx == ends - 1)
    def _():
        from_right[...] = jnp.zeros_like(from_right)

    for copy in loads[2:5]:
        copy.wait()

    def analyse(b, block):
        return jnp.dot(ana_ref[b % 4], jnp.concatenate([block, block], 0),
                       preferred_element_type=jnp.float32)

    def put(ref, at, row, value):
        high, low = split(value)
        ref[at, pl.ds(row, STEP), :] = high
        ref[at, pl.ds(256 + row, STEP), :] = low

    def synthesise(table, spectrum, at):
        terms = jnp.concatenate([spectrum[at], spectrum[at, pl.ds(0, 256), :]], 0)
        return jnp.dot(table, terms, preferred_element_type=jnp.float32)

    def own_tile(i, carry):
        for b in range(4):
            rows = pl.ds(b * REACH, REACH)
            g_block, x_block = gbuf[rows, cols(i)], xbuf[rows, cols(i)]
            if b > 0:
                x_block = x_block * live_ref[rows, :]
            if b in (1, 2):
                g_block = g_block * live_ref[rows, :]
            af[i, b + 1] = analyse(b + 1, g_block)
            xf[i, b] = analyse(b, x_block)

        for part in range(2):
            slot = 2 * (i - HALO_FROM) + part

            @pl.when(jnp.logical_and(slot >= 0, slot < tiles))
            def _(slot=slot):
                send_halo(slot)

        return carry

    lax.fori_loop(0, tiles, own_tile, None)
    for c in range(chunks):
        for d in range(Z - 1):
            taps_z(c, d).start()
    loads[1].wait()
    loads[5].wait()
    loads[6].wait()

    def windows(i, re, im):
        ar = [af[i, b, re, :] for b in range(6)]
        ai = [af[i, b, im, :] for b in range(6)]
        return [ar[b] + ar[b + 1] for b in range(5)], [ai[b] + ai[b + 1] for b in range(5)]

    def tap_tile(slot, carry):
        i = tile_at(slot)

        @pl.when(ctx > 0)
        def _():
            halo_right(i).wait_recv()

        @pl.when(ctx < ends - 1)
        def _():
            halo_left(i).wait_recv()

        af[i, 0] = analyse(0, from_left[i])
        af[i, 5] = analyse(5, from_right[i])

        def chunk(c, carry):
            row = pl.multiple_of(c * STEP, STEP)
            re, im = pl.ds(row, STEP), pl.ds(128 + row, STEP)
            gr, gi = windows(i, re, im)
            for h in range(2):
                tr = ti = None
                for b in range(4):
                    xr, xi = xf[i, b, re, :], xf[i, b, im, :]
                    pr = xr * gr[b + h] + xi * gi[b + h]
                    pi = xr * gi[b + h] - xi * gr[b + h]
                    tr, ti = (pr, pi) if tr is None else (tr + pr, ti + pi)
                put(tf, h, row, tr)
                put(tf, h, 128 + row, ti)
            return carry

        lax.fori_loop(0, 128 // STEP, chunk, None, unroll=True)
        for h in range(2):
            kind = jnp.where(i < x_first, 0, 1)
            terms = synthesise(tsyn_ref[kind, h], tf, h)
            for core_at in range(2):
                for u in range(4):
                    start = core_at * 64 + u * 16
                    unit = jnp.where(i < x_first, h * 4 + u, u * 2 + h)
                    tap[i, core_at, unit] = terms[start:start + 16]
        pair_copy(i).start()

        @pl.when(slot >= 2)
        def _():
            stage_pair(tile_at(slot - 2))


        return carry

    lax.fori_loop(0, tiles, tap_tile, None)
    stages = {"quarter": stage_quarter, "eighth": stage_eighth, "swap": stage_swap,
              "z": stage_z, "x": stage_x}
    plan = reduction_plan(tiles, x_first, chunks)

    stage_pair(tiles - 2)
    stage_pair(tiles - 1)
    for c in range(chunks):
        taps_to_x(c)
    for stage, tile in plan[chunks + 1]:
        stages[stage](tile)
    for c in range(chunks):
        taps_to_pair(c)
    for stage, tile in plan[chunks + 2]:
        stages[stage](tile)


    def weigh(i, at, spectrum):
        def chunk(c, carry):
            row = pl.multiple_of(c * STEP, STEP)
            re, im = pl.ds(row, STEP), pl.ds(128 + row, STEP)
            gr, gi = windows(i, re, im)
            w0r, w0i = wf[at, re, :], wf[at, im, :]
            w1r, w1i = wf[at + 1, re, :], wf[at + 1, im, :]
            for b in range(4):
                yr = (w0r * gr[b] + w0i * gi[b]) + (w1r * gr[b + 1] + w1i * gi[b + 1])
                yi = (w0r * gi[b] - w0i * gr[b]) + (w1r * gi[b + 1] - w1i * gr[b + 1])
                put(spectrum, b, row, yr)
                put(spectrum, b, 128 + row, yi)
            return carry

        lax.fori_loop(0, 128 // STEP, chunk, None, unroll=True)

    def emit(i, spectrum):
        for b in range(4):
            rows = pl.ds(b * REACH, REACH)
            value = synthesise(syn_ref[b], spectrum, b).astype(jnp.bfloat16)
            if b > 0:
                value = value * live_ref[rows, :]
            out_ref[0, rows, cols(i)] = value

    def grad_tiles(c, carry):
        taps_pair(c, 1 - core).wait_recv()
        first, second = 2 * c, 2 * c + 1
        for half, i in ((0, first), (1, second)):
            for h in range(2):
                block = wbuf[h, :, :, :, cols(i)].reshape(REACH, TILE)
                wf[half * 2 + h] = analyse(h, block)
        weigh(first, 0, ya)
        weigh(second, 2, yb)
        emit(first, ya)
        emit(second, yb)

        for at in range(chunks):
            @pl.when(c == at)
            def _(at=at):
                for stage, tile in plan[at]:
                    stages[stage](tile)

        return carry

    lax.fori_loop(0, chunks, grad_tiles, None)
    for stage, tile in plan[chunks]:
        stages[stage](tile)
    tap_out[...] = fin[...]

    def finish(i, carry):
        pair_copy(i).wait_send()

        @pl.when(i < x_first)
        def _():
            for d in range(3):
                quarter_copy(i, d).wait_send()
                eighth_copy(i, d).wait_send()
            swap_copy(i, rep).wait_send()

        @pl.when(i >= x_first)
        def _():
            for d in range(3):
                z_copy(i, d).wait_send()
                x_copy(i, d).wait_send()

        @pl.when(ctx < ends - 1)
        def _():
            halo_right(i).wait_send()

        @pl.when(ctx > 0)
        def _():
            halo_left(i).wait_send()

        return carry

    lax.fori_loop(0, tiles, finish, None)
    for c in range(chunks):
        for d in range(Z - 1):
            taps_z(c, d).wait_send()
        for d in range(2):
            taps_x(c, d, xlo).wait_send()
        taps_pair(c, core).wait_send()


def fused(counts, x, g, taps):
    _, rows, channels = x.shape
    tiles = channels // TILE
    ana, syn, tsyn = transform_tables()
    dma = pltpu.SemaphoreType.DMA
    hbm = pl.BlockSpec(memory_space=pl.ANY)
    f32, bf16 = jnp.float32, jnp.bfloat16
    vmem = pl.BlockSpec(memory_space=pltpu.VMEM)
    first, rest = X_FIRST, tiles - X_FIRST
    return pl.pallas_call(
        functools.partial(kernel, tiles),
        out_shape=(pltpu.VMEM(x.shape, bf16), pltpu.VMEM(taps.shape, f32)),
        in_specs=[pl.BlockSpec(memory_space=pltpu.SMEM)] + [hbm] * 6,
        out_specs=(vmem, vmem),
        scratch_shapes=[
            pltpu.VMEM(ana.shape, bf16),
            pltpu.VMEM(syn.shape, bf16),
            pltpu.VMEM(tsyn.shape, bf16),
            pltpu.VMEM((rows, TILE), bf16),
            pltpu.VMEM((rows, channels), bf16),
            pltpu.VMEM((rows, channels), bf16),
            pltpu.VMEM((tiles, REACH, TILE), bf16),
            pltpu.VMEM((tiles, REACH, TILE), bf16),
            pltpu.VMEM((2, Z, 2, 16, channels), bf16),
            pltpu.VMEM((tiles, 6, 256, TILE), f32),
            pltpu.VMEM((tiles, 4, 256, TILE), f32),
            pltpu.VMEM((4, 256, TILE), f32),
            pltpu.VMEM((4, 512, TILE), bf16),
            pltpu.VMEM((4, 512, TILE), bf16),
            pltpu.VMEM((2, 512, TILE), bf16),
            pltpu.VMEM((tiles, 2, 8, 16, TILE), f32),
            pltpu.VMEM((tiles, 8, 16, TILE), f32),
            pltpu.VMEM((first, 3, 2, 16, TILE), f32),
            pltpu.VMEM((first, 3, 8, TILE), f32),
            pltpu.VMEM((rest, 3, 2, 16, TILE), f32),
            pltpu.VMEM((rest, 3, 16, TILE), f32),
            pltpu.VMEM((16, channels), f32),
            dma((8,)),
            dma((2, tiles)), dma((2, tiles)),
            dma((tiles // 2, 3)), dma((tiles // 2, 3)),
            dma((tiles // 2, 2)), dma((tiles // 2, 2)),
            dma((tiles // 2,)), dma((tiles // 2,)),
            dma((tiles,)), dma((tiles,)),
            dma((first, 3)), dma((first, 3)),
            dma((first, 3)), dma((first, 3)),
            dma((first,)), dma((first,)),
            dma((rest, 3)), dma((rest, 3)),
            dma((rest, 3)), dma((rest, 3)),
        ],
        compiler_params=pltpu.CompilerParams(
            collective_id=0, has_side_effects=True, vmem_limit_bytes=56 << 20),
    )(counts, jnp.asarray(ana), jnp.asarray(syn), jnp.asarray(tsyn), x, g, taps)


def local(saved_input, out_grad, filter_taps, valid_counts):
    return fused(valid_counts, saved_input, out_grad, filter_taps)


def solution(mesh):
    return jax.shard_map(
        local,
        mesh=mesh,
        in_specs=(P("rep", "ctx", "ch"), P("rep", "ctx", "ch"), P("ctx", "ch"), P("rep", "ctx")),
        out_specs=(P("rep", "ctx", "ch"), P("ctx", "ch")),
        check_vma=False,
    )
```
